32 devices in a mesh: wl: 4 (over x, core), gx: 2 (over y), gy: 4 (over z).
Axes of the slice: x: 2, y: 2, z: 4, core: 2. Of those that a mesh axis runs over, the one named last changes fastest.
Arguments:
- forward_efield: float32 [4, 3, 64, 32, 128], P('wl', None, 'gx', 'gy'), may hold values from -6 to 6
- forward_hfield: float32 [4, 3, 64, 32, 128], P('wl', None, 'gx', 'gy'), may hold values from -6 to 6
- adjoint_efield: float32 [4, 3, 64, 32, 128], P('wl', None, 'gx', 'gy'), may hold values from -6 to 6
- adjoint_hfield: float32 [4, 3, 64, 32, 128], P('wl', None, 'gx', 'gy'), may hold values from -6 to 6
- background: float32 [64, 32, 128], P('gx', 'gy'), may hold values from 1 to 4
- design: float32 [8, 64, 32], P('wl', 'gx', 'gy'), may hold values from 1.5 to 6
- source_profile: float32 [4, 64, 32], P('wl', 'gx', 'gy'), may hold values from -24 to 24
- source_layer: int32 [4], P('wl'), may hold values from 4 to 59
- monitor_layer: int32 [4], P('wl'), may hold values from 76 to 123
Outputs:
- final_forward: float32 [4, 3, 64, 32, 128], P('wl', None, 'gx', 'gy')
- final_adjoint: float32 [4, 3, 64, 32, 128], P('wl', None, 'gx', 'gy')
- gradient: float32 [8, 64, 32], P('wl', 'gx', 'gy')
The draws below stay inside these ranges and needn't reach their ends.
Inputs may be any that keep to these rules, and one draw needn't show every extreme that they name: `source_layer`: a z layer below the design slab. `monitor_layer`: a z layer above the design slab.
All inputs are finite; a program needn't handle non-finite values.
Results may differ from the reference program's by a relative error of at most 0.0001.
Values sent between devices are 32-bit elements; how exact they have to be, the bound alone decides.
No kernel may reach another device: no remote copies, remote signals or barrier semaphores. Data moves between devices by JAX's collectives and lax.ppermute only.
A program may use at most 64 MiB of HBM per device.

```python
import math
import jax
import jax.numpy as jnp
from jax import lax

NZ = 128
Z0 = 64
STEPS = 3
DL = 8
WL = 4
NX = 64
NY = 32


def place_ends(values, own_key, low, largest):
    longest = values.shape.index(max(values.shape))
    spots = []
    for shift in (0, 1):
        where = [jax.random.randint(jax.random.fold_in(own_key, axis), (), 0, length) for axis, length in enumerate(values.shape)]
        where[longest] = (where[longest] + shift) % values.shape[longest]
        spots.append(tuple(where))
    return values.at[spots[0]].set(low).at[spots[1]].set(largest)


def block_levels(rng, shape, cuts, least, largest):
    gain, own = 1.0, jax.random.fold_in(rng, 6)
    for axis_at, parts in cuts:
        draws = jnp.exp(jax.random.uniform(jax.random.fold_in(own, axis_at), (parts,), jnp.float32, least / len(cuts), largest / len(cuts)))
        gain = gain * jnp.repeat(draws, shape[axis_at] // parts).reshape([-1 if axis == axis_at else 1 for axis in range(len(shape))])
    return gain


def bell_draw(own_key, dims, scale, bound, cuts=(), held_as=jnp.bfloat16):
    values = jax.random.normal(own_key, dims, jnp.float32) * scale
    if len(cuts) > 0:
        values = block_levels(own_key, dims, cuts, -0.22, 0.18) * values
    return jnp.clip(values, min=-bound, max=bound).astype(held_as)


def setup_inputs(seed: int = 0) -> dict:
    key_list = jax.random.split(jax.random.key(seed), 10)
    forward_efield = bell_draw(key_list[0], (WL, 3, NX, NY, NZ), 1.0, 6.0, ((0, 4), (2, 2), (3, 4)), jnp.float32)
    forward_hfield = bell_draw(key_list[1], (WL, 3, NX, NY, NZ), 1.0, 6.0, ((0, 4), (2, 2), (3, 4)), jnp.float32)
    adjoint_efield = bell_draw(key_list[2], (WL, 3, NX, NY, NZ), 1.0, 6.0, ((0, 4), (2, 2), (3, 4)), jnp.float32)
    adjoint_hfield = bell_draw(key_list[3], (WL, 3, NX, NY, NZ), 1.0, 6.0, ((0, 4), (2, 2), (3, 4)), jnp.float32)
    background = jnp.clip(1.0 + 3.0 * jax.random.uniform(key_list[4], (NX, NY, NZ), jnp.float32) ** block_levels(key_list[4], (NX, NY, NZ), ((0, 2), (1, 4)), -0.2, 0.2), 1.0, 4.0)
    design = jnp.clip(1.5 + 4.5 * jax.random.uniform(key_list[5], (DL, NX, NY), jnp.float32) ** block_levels(key_list[5], (DL, NX, NY), ((0, 4), (1, 2), (2, 4)), -0.2, 0.2), 1.5, 6.0)
    source_profile = bell_draw(key_list[6], (WL, NX, NY), 4.0, 24.0, ((0, 4), (1, 2), (2, 4)), jnp.float32)
    source_layer = place_ends(jax.random.randint(key_list[7], (WL,), 4, Z0 - 4), jax.random.fold_in(key_list[7], 1), 4, (Z0 - 4) - 1).astype(jnp.int32)
    monitor_layer = place_ends(jax.random.randint(key_list[8], (WL,), Z0 + DL + 4, NZ - 4), jax.random.fold_in(key_list[8], 1), Z0 + DL + 4, (NZ - 4) - 1).astype(jnp.int32)
    return dict(forward_efield=forward_efield, forward_hfield=forward_hfield, adjoint_efield=adjoint_efield, adjoint_hfield=adjoint_hfield, background=background, design=design, source_profile=source_profile, source_layer=source_layer, monitor_layer=monitor_layer)


time_step = 0.5


def along(stacked, axis, edge, upward):
    count = stacked.shape[axis]
    if upward:
        shifted = jnp.concatenate([lax.slice_in_dim(stacked, 1, count, axis=axis), edge], axis=axis)
        return shifted - stacked
    shifted = jnp.concatenate([edge, lax.slice_in_dim(stacked, 0, count - 1, axis=axis)], axis=axis)
    return stacked - shifted


def curl(stacked, upward):
    comps, width, height, depth = stacked.shape
    edge_x = jnp.zeros((comps, 1, height, depth), jnp.float32)
    edge_y = jnp.zeros((comps, width, 1, depth), jnp.float32)
    edge_z = jnp.zeros((comps, width, height, 1), jnp.float32)
    along_x = along(stacked, 1, edge_x, upward)
    along_y = along(stacked, 2, edge_y, upward)
    along_z = along(stacked, 3, edge_z, upward)
    return jnp.stack([along_y[2] - along_z[1], along_z[0] - along_x[2], along_x[1] - along_y[0]])


def reference(forward_efield, forward_hfield, adjoint_efield, adjoint_hfield, background, design, source_profile, source_layer, monitor_layer):
    permit = jnp.concatenate([background[:, :, :Z0], jnp.transpose(design, (1, 2, 0)), background[:, :, Z0 + DL:]], axis=2)
    coef = time_step / permit
    layers = lax.iota(jnp.int32, NZ)
    outs_forward = []
    outs_adjoint = []
    gradient = jnp.zeros((DL, NX, NY), jnp.float32)
    for wave_index in range(WL):
        omega = jnp.float32(2.0 * math.pi) / (16.0 + 32.0 * jnp.asarray(wave_index, jnp.float32) / WL)
        source_mask = (layers == source_layer[wave_index]).astype(jnp.float32)
        monitor_mask = (layers == monitor_layer[wave_index]).astype(jnp.float32)
        efield = forward_efield[wave_index]
        hfield = forward_hfield[wave_index]
        slabs = []
        monitors = []
        for turn in range(STEPS):
            hfield = hfield - time_step * curl(efield, True)
            efield = efield + coef * curl(hfield, False)
            signal = jnp.sin(omega * ((turn + 1) * time_step))
            efield = efield.at[0].add(time_step * signal * source_profile[wave_index][:, :, None] * source_mask)
            slabs.append(efield[:, :, :, Z0:Z0 + DL])
            monitors.append(lax.dynamic_slice_in_dim(efield, monitor_layer[wave_index].astype(jnp.int32), 1, 3))
        outs_forward.append(efield)
        adj_e = adjoint_efield[wave_index]
        adj_h = adjoint_hfield[wave_index]
        total = jnp.zeros((NX, NY, DL), jnp.float32)
        for turn in range(STEPS):
            adj_h = adj_h - time_step * curl(adj_e, True)
            adj_e = adj_e + coef * curl(adj_h, False)
            adj_e = adj_e + (2.0 * time_step) * monitors[STEPS - 1 - turn] * monitor_mask
            total = total + jnp.sum(slabs[STEPS - 1 - turn] * adj_e[:, :, :, Z0:Z0 + DL], axis=0)
        outs_adjoint.append(adj_e)
        gradient = gradient + jnp.transpose(omega * omega * total, (2, 0, 1))
    return jnp.stack(outs_forward), jnp.stack(outs_adjoint), gradient
```

```python
import math

import jax
import jax.numpy as jnp
import numpy as np
from jax import lax
from jax.experimental import pallas as pl
from jax.experimental.pallas import tpu as pltpu
from jax.sharding import PartitionSpec as P

Z0 = 64
STEPS = 3
DT = 0.5
F32 = jnp.float32
FH = 5
AH = 3
CH = 4


def pair(axis, parity):
    def go(i):
        return (i ^ 1) if parity == 0 else ((i + 1) ^ 1) - 1
    return go


def swap(block, flip_x, parity):
    nx, ny = lax.axis_size("gx"), lax.axis_size("gy")
    go = (lambda i: i) if parity is None else pair("gy", parity)
    route = []
    for a in range(nx):
        for b in range(ny):
            ta, tb = (a ^ 1 if flip_x else a), go(b)
            if 0 <= ta < nx and 0 <= tb < ny:
                route.append((a * ny + b, ta * ny + tb))
    return lax.ppermute(block, ("gx", "gy"), route)


def y_units():
    units = [("fe", c, s) for c in range(3) for s in range(FH)]
    units += [("fh", c, s) for c in range(3) for s in range(FH)]
    units += [("ae", c, s) for c in range(3) for s in range(AH)]
    units += [("ah", c, s) for c in range(3) for s in range(AH)]
    units += [("co", 0, s) for s in range(CH)]
    return units


def x_units(ny):
    units = [(a, c, y) for a in ("fe", "fh", "ae", "ah") for c in range(3) for y in range(ny)]
    return units + [("co", 0, y) for y in range(ny)]


def dims(xl, yl):
    return xl + 8, yl + 2 * FH


def pack_body(fe, fh, ae, ah, bg, dsg, sp, co, pa, pb, px, pda, pdb, *, xl, yl):
    depth = dsg.shape[0]
    gx, gy = lax.axis_index("gx"), lax.axis_index("gy")
    lane = lax.broadcasted_iota(jnp.int32, (xl, 128), 1)
    layers = [dsg[l] for l in range(depth)]
    for y in range(yl):
        perm = bg[pl.ds(y, xl, stride=yl), :]
        for l in range(depth):
            col = jnp.broadcast_to(layers[l][:, y : y + 1], (xl, 128))
            perm = jnp.where(lane == Z0 + l, col, perm)
        co[y] = DT / perm
    refs = dict(fe=fe, fh=fh, ae=ae, ah=ah)
    x0 = pl.multiple_of(jnp.where(gx == 0, xl - 8, 0), 8)
    prof = sp[...]
    zero = jnp.zeros((xl, 128), F32)
    plane = xl * yl
    for dst, dst_d, up in ((pa, pda, gy % 2 == 0), (pb, pdb, gy % 2 == 1)):
        base = dict(fe=FH, fh=FH, ae=AH, ah=AH, co=CH)
        base = {k: jnp.where(up, yl - v, 0) for k, v in base.items()}
        u = 0
        for name, c, s in y_units():
            row = base[name] + s
            if name == "co":
                dst[u] = co[row]
            else:
                dst[u] = refs[name][pl.ds(c * plane + row, xl, stride=yl), :]
            u += 1
        dst[u] = zero
        dst[u, :, 0:FH] = jnp.where(up, prof[:, yl - FH : yl], prof[:, 0:FH])
        for v in range(u + 1):
            dst_d[v] = dst[v, pl.ds(x0, 8), :]
    u = 0
    for name, c, y in x_units(yl):
        if name == "co":
            px[u] = co[y, pl.ds(x0, 8), :]
        else:
            px[u] = refs[name][pl.ds(c * plane + x0 * yl + y, 8, stride=yl), :]
        u += 1
    px[u] = jnp.zeros((8, 128), F32)
    px[u, :, 0:yl] = sp[pl.ds(x0, 8), :]


def main_body(fe, fh, ae, ah, co, sp, ra, rb, rx, rda, rdb, src, mon, out_f, out_a, grad,
              e0, e1, e2, e3, h, a, g, cx, sx, *, xl, yl, nw, signals, omegas):
    xr, yr = dims(xl, yl)
    gx, gy, w = lax.axis_index("gx"), lax.axis_index("gy"), lax.axis_index("wl")
    lane = lax.broadcasted_iota(jnp.int32, (xr, 128), 1)
    sub = lax.broadcasted_iota(jnp.int32, (8, 128), 0)
    src_l, mon_l = src[0], mon[0]
    keep = jnp.where(gx == 0, (sub < FH).astype(F32), (sub >= 8 - FH).astype(F32))
    big = dict(fe=e0, fh=h, ae=a, ah=g)
    plane = xl * yl
    halo = pl.ds(xl, 8)
    own = pl.ds(0, xl)
    for name, ref in (("fe", fe), ("fh", fh), ("ae", ae), ("ah", ah)):
        for c in range(3):
            for y in range(yl):
                big[name][c, FH + y, own, :] = ref[pl.ds(c * plane + y, xl, stride=yl), :]
    for y in range(yl):
        cx[FH + y, own, :] = co[y]
    at_src = lax.broadcasted_iota(jnp.int32, (xl, 128), 1) == src_l
    at_src8 = lax.broadcasted_iota(jnp.int32, (8, 128), 1) == src_l
    zero, zero8 = jnp.zeros((xl, 128), F32), jnp.zeros((8, 128), F32)
    prof = sp[...]
    u = 0
    for name, c, y in x_units(yl):
        tile = rx[u] * keep
        if name == "co":
            cx[FH + y, halo, :] = tile
        else:
            big[name][c, FH + y, halo, :] = tile
        u += 1
    prof_x = rx[u] * keep
    for y in range(yl):
        sx[FH + y, own, :] = jnp.where(at_src, jnp.broadcast_to(prof[:, y : y + 1], (xl, 128)), zero)
        sx[FH + y, halo, :] = jnp.where(at_src8, jnp.broadcast_to(prof_x[:, y : y + 1], (8, 128)), zero8)
    for ref, ref_d, high in ((ra, rda, gy % 2 == 0), (rb, rdb, gy % 2 == 1)):
        first = {}
        for name, deep in (("fe", FH), ("fh", FH), ("ae", AH), ("ah", AH), ("co", CH)):
            first[name] = jnp.where(high, FH + yl, FH - deep)
        u = 0
        for name, c, s in y_units():
            row = first[name] + s
            tile = ref_d[u] * keep
            if name == "co":
                cx[row, own, :] = ref[u]
                cx[row, halo, :] = tile
            else:
                big[name][c, row, own, :] = ref[u]
                big[name][c, row, halo, :] = tile
            u += 1
        prof_y, prof_d = ref[u], ref_d[u] * keep
        for s in range(FH):
            row = first["fe"] + s
            sx[row, own, :] = jnp.where(at_src, jnp.broadcast_to(prof_y[:, s : s + 1], (xl, 128)), zero)
            sx[row, halo, :] = jnp.where(at_src8, jnp.broadcast_to(prof_d[:, s : s + 1], (8, 128)), zero8)

    ring = lax.broadcasted_iota(jnp.int32, (xr, 128), 0)
    inside_low = jnp.where(ring < xl + FH, F32(DT), F32(0.0))
    inside_high = jnp.where((ring < xl) | (ring >= xr - FH), F32(DT), F32(0.0))
    h_in = jnp.where(gx == 0, inside_low, inside_high)
    low = jnp.where(gy == 0, 0.0, 1.0).astype(F32)
    h_low = h_in * low
    z_last = lane == 127
    z_first = lane == 0
    at_mon = lane == mon_l

    def zup(v):
        return jnp.where(z_last, 0.0, pltpu.roll(v, 127, 1)) - v

    def zdn(v):
        return v - jnp.where(z_first, 0.0, pltpu.roll(v, 1, 1))

    def xup(v):
        return pltpu.roll(v, xr - 1, 0) - v

    def xdn(v):
        return v - pltpu.roll(v, 1, 0)

    def step_h(e, hh, y):
        k = h_low if y < FH else h_in
        ex, ey, ez = e[0, y], e[1, y], e[2, y]
        hh[0, y] = hh[0, y] - k * ((e[2, y + 1] - ez) - zup(ey))
        hh[1, y] = hh[1, y] - k * (zup(ex) - xup(ez))
        hh[2, y] = hh[2, y] - k * (xup(ey) - (e[0, y + 1] - ex))

    def curl_e(hh, y):
        hx, hy, hz = hh[0, y], hh[1, y], hh[2, y]
        k = cx[y]
        return (
            k * ((hz - hh[2, y - 1]) - zdn(hy)),
            k * (zdn(hx) - xdn(hz)),
            k * (xdn(hy) - (hx - hh[0, y - 1])),
        )

    def pick(values):
        value = F32(values[0])
        for i in range(1, nw):
            value = jnp.where(w == i, F32(values[i]), value)
        return value

    runs = (e0, e1, e2, e3)
    for k in range(STEPS):
        old, new = runs[k], runs[k + 1]
        signal = pick([signals[i][k] for i in range(nw)])
        for y in range(k, yr - 1 - k):
            step_h(old, h, y)
            if y > k:
                dx, dy, dz = curl_e(h, y)
                new[0, y] = old[0, y] + dx + signal * sx[y]
                new[1, y] = old[1, y] + dy
                new[2, y] = old[2, y] + dz
    total = [None] * yl
    for j in range(STEPS):
        seen = runs[STEPS - j]
        for y in range(FH - AH + j, yr - AH - j):
            step_h(a, g, y)
            if y > FH - AH + j:
                for c, d in enumerate(curl_e(g, y)):
                    f = seen[c, y]
                    v = a[c, y] + d + jnp.where(at_mon, 2.0 * DT * f, 0.0)
                    a[c, y] = v
                    if FH <= y < FH + yl:
                        t = (f * v)[0:xl]
                        i = y - FH
                        total[i] = t if total[i] is None else total[i] + t
    lane_o = lax.broadcasted_iota(jnp.int32, (xl, 128), 1)
    scale = pick([o * o for o in omegas])
    packed = jnp.zeros((xl, 128), F32)
    wide = 128 // yl
    for y in range(yl):
        moved = pltpu.roll(total[y] * scale, (wide * y - Z0) % 128, 1)
        packed = jnp.where((lane_o >= wide * y) & (lane_o < wide * y + wide), moved, packed)
    grad[...] = packed
    for c in range(3):
        for y in range(yl):
            out_f[pl.ds(c * plane + y, xl, stride=yl), :] = e3[c, FH + y, own, :]
            out_a[pl.ds(c * plane + y, xl, stride=yl), :] = a[c, FH + y, own, :]


def sum_body(*refs, owned, yl):
    *parts, out = refs
    w = lax.axis_index("wl")
    acc = parts[0][...]
    for p in parts[1:]:
        acc = acc + p[...]
    acc = pltpu.roll(acc, (128 - owned * w) % 128, 1)
    lane = lax.broadcasted_iota(jnp.int32, acc.shape, 1)
    wide = 128 // yl
    for i in range(owned):
        res = jnp.zeros_like(acc)
        for y in range(yl):
            res = jnp.where(lane == y, pltpu.roll(acc, (y - wide * y - i) % 128, 1), res)
        out[i] = res[:, 0:yl]


def per_device(fe, fh, ae, ah, background, design, source_profile, source_layer, monitor_layer):
    _, _, xl, yl, nz = fe.shape
    nw = lax.axis_size("wl")
    owned = design.shape[0]
    flat = [v.reshape(3 * xl * yl, nz) for v in (fe, fh, ae, ah)]
    bg = background.reshape(xl * yl, nz)
    sp = source_profile[0]
    tiles = lax.all_gather(design, "wl", axis=0, tiled=True)
    xr, yr = dims(xl, yl)
    n_y, n_x = len(y_units()) + 1, len(x_units(yl)) + 1
    shape = lambda *s: jax.ShapeDtypeStruct(s, F32)
    params = pltpu.CompilerParams(vmem_limit_bytes=50 * 1024 * 1024)
    co, pa, pb, px, pda, pdb = pl.pallas_call(
        lambda *r: pack_body(*r, xl=xl, yl=yl),
        out_shape=(shape(yl, xl, nz), shape(n_y, xl, nz), shape(n_y, xl, nz), shape(n_x, 8, nz),
                   shape(n_y, 8, nz), shape(n_y, 8, nz)),
        compiler_params=params,
        name="pack",
    )(*flat, bg, tiles, sp)
    ra = swap(pa, False, 0)
    rb = swap(pb, False, 1)
    rx = swap(px, True, None)
    rda = swap(pda, True, 0)
    rdb = swap(pdb, True, 1)
    f32 = np.float32
    omegas = [f32(2.0 * math.pi) / (f32(16.0) + f32(32.0) * f32(i) / f32(nw)) for i in range(nw)]
    signals = [[f32(DT) * np.sin(f32(o * f32((k + 1) * DT))) for k in range(STEPS)] for o in omegas]
    ext = lambda *s: pltpu.VMEM(s, F32)
    field = ext(3, yr, xr, nz)
    smem = pl.BlockSpec(memory_space=pltpu.SMEM)
    out_f, out_a, grad = pl.pallas_call(
        lambda *r: main_body(*r, xl=xl, yl=yl, nw=nw, signals=signals, omegas=omegas),
        out_shape=(shape(3 * xl * yl, nz), shape(3 * xl * yl, nz), shape(xl, nz)),
        in_specs=[pl.BlockSpec(memory_space=pltpu.VMEM)] * 11 + [smem, smem],
        scratch_shapes=[field] * 7 + [ext(yr, xr, nz), ext(yr, xr, nz)],
        compiler_params=params,
        name="window",
    )(*flat, co, sp, ra, rb, rx, rda, rdb, source_layer, monitor_layer)
    parts = [grad]
    for k in range(1, nw):
        parts.append(lax.ppermute(grad, "wl", [(i, i ^ k) for i in range(nw)]))
    gradient = pl.pallas_call(
        lambda *r: sum_body(*r, owned=owned, yl=yl),
        out_shape=shape(owned, xl, yl),
        compiler_params=params,
        name="gather_sum",
    )(*parts)
    block = (1, 3, xl, yl, nz)
    return (out_f.reshape(block), out_a.reshape(block), gradient)


def solution(mesh):
    field = P("wl", None, "gx", "gy", None)
    return jax.shard_map(
        per_device,
        mesh=mesh,
        in_specs=(field, field, field, field, P("gx", "gy", None), P("wl", "gx", "gy"),
                  P("wl", "gx", "gy"), P("wl"), P("wl")),
        out_specs=(field, field, P("wl", "gx", "gy")),
        check_vma=False,
    )
```

```python
import math

import jax
import jax.numpy as jnp
import numpy as np
from jax import lax
from jax.experimental import pallas as pl
from jax.experimental.pallas import tpu as pltpu
from jax.sharding import PartitionSpec as P

Z0 = 64
STEPS = 3
DT = 0.5
F32 = jnp.float32
BF16 = jnp.bfloat16
FH = 5
AH = 3
WIN = 16
PER = 128 // WIN
PROF = 112


def swap(block, flip_x, parity):
    nx, ny = lax.axis_size("gx"), lax.axis_size("gy")
    route = []
    for a in range(nx):
        for b in range(ny):
            ta = a ^ 1 if flip_x else a
            tb = b if parity is None else ((b + parity) ^ 1) - parity
            if 0 <= ta < nx and 0 <= tb < ny:
                route.append((a * ny + b, ta * ny + tb))
    return lax.ppermute(block, ("gx", "gy"), route)


FWD, ADJ = ("fe", "fh"), ("ae", "ah")
F_RAW = [(n, c, i) for n in FWD for c in range(3) for i in range(AH)] + [("co", 0, i) for i in range(2)]
A_RAW = [(n, c, i) for n in ADJ for c in range(3) for i in range(AH)]
F_WIN = [(n, c, i) for n in FWD for c in range(3) for i in range(AH, FH)] + [("co", 0, i) for i in (2, 3)]
C_RAW = [(n, c, i) for n in FWD + ADJ for c in range(3) for i in range(AH)] + [("co", 0, i) for i in range(2)]
C_WIN = [(n, c, i) for n in FWD for c in range(3) for i in range(FH)] + [("co", 0, i) for i in range(4)]


def x_parts(yl):
    raw = [(n, c, y) for n in FWD + ADJ for c in range(3) for y in range(yl)]
    win = [(n, c, y) for n in FWD for c in range(3) for y in range(yl)]
    co = [("co", 0, y) for y in range(yl)]
    return raw + co, win + co


def ceil(a, b):
    return -(-a // b)


def fetch_body(*refs):
    n = len(refs) // 2
    ins, outs, sems = refs[:n], refs[n : 2 * n], refs[2 * n]
    copies = [pltpu.make_async_copy(s, d, sems.at[i]) for i, (s, d) in enumerate(zip(ins, outs))]
    for c in copies:
        c.start()
    for c in copies:
        c.wait()


def send_body(mon, fe, fh, ae, ah, bg, sp, *rest, xl, yl, nw, owned):
    parts, (co, prof_t, fa, fb, aa, ab, px, da, db, turn) = rest[:nw], rest[nw:]
    gx, gy, w = lax.axis_index("gx"), lax.axis_index("gy"), lax.axis_index("wl")
    plane = xl * yl
    depth = nw * owned
    lane = lax.broadcasted_iota(jnp.int32, (xl, 128), 1)
    lane8 = lane[0:8]
    first = WIN // 2 - mon[0] + 256
    refs = dict(fe=fe, fh=fh, ae=ae, ah=ah)
    turn[...] = jnp.zeros((128, 128), F32)
    for k in range(nw):
        for i in range(owned):
            turn[pl.ds(owned * (w ^ k) + i, yl, stride=depth), 0:xl] = parts[k][i]
    layers = jnp.transpose(turn[...])[0:xl]
    for y in range(yl):
        moved = pltpu.roll(layers, (Z0 - depth * y) % 128, 1)
        perm = jnp.where((lane >= Z0) & (lane < Z0 + depth), moved, bg[pl.ds(y, xl, stride=yl), :])
        co[y] = DT / perm
    turn[0:yl, 0:xl] = sp[...]
    prof_t[...] = jnp.transpose(turn[...])[0:xl]
    low_x = gx == 0
    x8 = pl.multiple_of(jnp.where(low_x, xl - 8, 0), 8)
    x4 = jnp.where(low_x, xl - 4, 0)

    def rows(name, c, r, x, count):
        if name == "co":
            return co[r, pl.ds(x, count), :]
        return refs[name][pl.ds(c * plane + x * yl + r, count, stride=yl), :]

    def windows(parts, x, count, where):
        out = []
        here = lax.broadcasted_iota(jnp.int32, (count, 128), 1)
        for t in range(ceil(len(parts), PER)):
            acc = jnp.zeros((count, 128), F32)
            for q, (name, c, i) in enumerate(parts[t * PER : (t + 1) * PER]):
                moved = pltpu.roll(rows(name, c, where(i), x, count), (WIN * q + first) % 128, 1)
                acc = jnp.where((here >= WIN * q) & (here < WIN * (q + 1)), moved, acc)
            out.append(acc)
        return out

    def tiles(dst, raw, win, where):
        for n, (name, c, i) in enumerate(raw):
            if name == "co":
                part = pltpu.roll(rows(name, c, where(i), x8, 8), jnp.where(low_x, 4, 0), 0)[0:4]
            else:
                part = rows(name, c, where(i), x4, 4)
            dst[n // 2, 4 * (n % 2) : 4 * (n % 2) + 4, :] = part
        at = ceil(len(raw), 2)
        for tile in windows(win, x8, 8, where):
            dst[at] = tile
            at += 1
        return at

    for dst, dst_a, corner, up in ((fa, aa, da, gy % 2 == 0), (fb, ab, db, gy % 2 == 1)):
        where = lambda i, up=up: jnp.where(up, yl - 1 - i, i)
        for u, (name, c, i) in enumerate(F_RAW):
            dst[u] = rows(name, c, where(i), 0, xl)
        for u, (name, c, i) in enumerate(A_RAW):
            dst_a[u] = rows(name, c, where(i), 0, xl)
        at = len(F_RAW)
        for unit in windows(F_WIN, 0, xl, where):
            dst[at] = unit
            at += 1
        mix = dst[at - 1]
        prof = prof_t[...]
        for i in range(FH):
            col = jnp.where(up, prof[:, yl - 1 - i : yl - i], prof[:, i : i + 1])
            mix = jnp.where(lane == PROF + i, jnp.broadcast_to(col, (xl, 128)), mix)
        dst[at - 1] = mix
        last = tiles(corner, C_RAW, C_WIN, where)
        src8 = dst[at - 1, pl.ds(x8, 8), :]
        corner[last - 1] = jnp.where((lane8 >= PROF) & (lane8 < PROF + FH), src8, corner[last - 1])
    raw, win = x_parts(yl)
    last = tiles(px, raw, win, lambda y: y)
    px[last] = prof_t[pl.ds(x8, 8), :]


class Halo:
    def __init__(self, mon, xl, yl, put):
        self.xl, self.yl, self.put = xl, yl, put
        self.gx, self.gy = lax.axis_index("gx"), lax.axis_index("gy")
        self.back = mon - WIN // 2 + 256
        sub = lax.broadcasted_iota(jnp.int32, (8, 128), 0)
        low = self.gx == 0
        mask = lambda lo, hi: jnp.where(low, lo.astype(F32), hi.astype(F32))
        self.keep = mask(sub < FH, sub >= 8 - FH)
        self.near = mask(sub < 4, sub >= 4) > 0.5
        self.far = mask((sub >= 4) & (sub < FH), (sub < 4) & (sub >= 8 - FH)) > 0.5
        self.shift = [jnp.where(low, 0, 4), jnp.where(low, 4, 0)]

    def row(self, i, high):
        return jnp.where(high, FH + self.yl + i, FH - 1 - i)

    def unroll(self, tile, q):
        return pltpu.roll(tile, (self.back - WIN * q) % 128, 1)

    def side(self, ref, raw, win, high):
        own = pl.ds(0, self.xl)
        for u, (name, c, i) in enumerate(raw):
            self.put(name, c, self.row(i, high), own, ref[u])
        for s, (name, c, i) in enumerate(win):
            self.put(name, c, self.row(i, high), own, self.unroll(ref[len(raw) + s // PER], s % PER))

    def tiles(self, ref, raw, win, names, where):
        halo = pl.ds(self.xl, 8)
        seats = {part: s for s, part in enumerate(win)}
        at = ceil(len(raw), 2)
        for n, part in enumerate(raw):
            if part[0] not in names:
                continue
            value = jnp.where(self.near, pltpu.roll(ref[n // 2], self.shift[n % 2], 0), 0.0)
            if part in seats:
                s = seats.pop(part)
                value = jnp.where(self.far, self.unroll(ref[at + s // PER], s % PER), value)
            self.put(part[0], part[1], where(part[2]), halo, value)
        for part, s in seats.items():
            if part[0] in names:
                self.put(part[0], part[1], where(part[2]), halo, self.unroll(ref[at + s // PER], s % PER) * self.keep)


class Stepper:
    def __init__(self, xl, yl, cx):
        self.xr = xr = xl + 8
        self.cx = cx
        gx, gy = lax.axis_index("gx"), lax.axis_index("gy")
        self.lane = lax.broadcasted_iota(jnp.int32, (xr, 128), 1)
        ring = lax.broadcasted_iota(jnp.int32, (xr, 128), 0)
        inside_low = jnp.where(ring < xl + FH, F32(DT), F32(0.0))
        inside_high = jnp.where((ring < xl) | (ring >= xr - FH), F32(DT), F32(0.0))
        self.h_in = jnp.where(gx == 0, inside_low, inside_high)
        self.h_low = self.h_in * jnp.where(gy == 0, 0.0, 1.0).astype(F32)
        self.z_last = self.lane == 127
        ri = lax.broadcasted_iota(jnp.int32, (128, 128), 0)
        ci = lax.broadcasted_iota(jnp.int32, (128, 128), 1)
        diff = jnp.where(ri == ci, F32(1.0), F32(0.0)) - jnp.where(ri == ci - 1, F32(1.0), F32(0.0))
        self.diff = jnp.concatenate([diff] * 3, 0).astype(BF16)

    def zdn(self, p, q):
        v = jnp.concatenate([p, q], 0)
        hi = v.astype(BF16)
        rest = v - hi.astype(F32)
        mid = rest.astype(BF16)
        low = (rest - mid.astype(F32)).astype(BF16)
        out = lax.dot_general(jnp.concatenate([hi, mid, low], 1), self.diff, (((1,), (0,)), ((), ())),
                              preferred_element_type=F32)
        return out[0 : self.xr], out[self.xr :]

    def zup(self, v):
        return jnp.where(self.z_last, 0.0, pltpu.roll(v, 127, 1)) - v

    def xup(self, v):
        return pltpu.roll(v, self.xr - 1, 0) - v

    def xdn(self, v):
        return v - pltpu.roll(v, 1, 0)

    def rows(self, e, h, start, stop):
        load = lambda ref, y: (ref[0, y], ref[1, y], ref[2, y])
        cur, now = load(e, start), None
        for y in range(start, stop):
            up = load(e, y + 1)
            below = now
            k = self.h_low if y < FH else self.h_in
            ex, ey, ez = cur
            now = (
                h[0, y] - k * ((up[2] - ez) - self.zup(ey)),
                h[1, y] - k * (self.zup(ex) - self.xup(ez)),
                h[2, y] - k * (self.xup(ey) - (up[0] - ex)),
            )
            for c in range(3):
                h[c, y] = now[c]
            if y > start:
                hx, hy, hz = now
                k = self.cx[y]
                zy, zx = self.zdn(hy, hx)
                yield y, cur, (
                    k * ((hz - below[2]) - zy),
                    k * (zx - self.xdn(hz)),
                    k * (self.xdn(hy) - (hx - below[0])),
                )
            cur = up


def pick(values):
    w = lax.axis_index("wl")
    value = F32(values[0])
    for i in range(1, len(values)):
        value = jnp.where(w == i, F32(values[i]), value)
    return value


def fill_own(refs, bigs, xl, yl):
    for ref, big in zip(refs, bigs):
        for c in range(3):
            for y in range(yl):
                big[c, FH + y, 0:xl, :] = ref[pl.ds(c * xl * yl + y, xl, stride=yl), :]


def put_out(big, out, xl, yl):
    for c in range(3):
        for y in range(yl):
            out[pl.ds(c * xl * yl + y, xl, stride=yl), :] = big[c, FH + y, 0:xl, :]


def forward_body(src, mon, fe, fh, co, prof_t, ra, rb, rx, rda, rdb, out, cx, e1, e2, e3, e0, h, sx, *, xl, yl, signals):
    xr, yr = xl + 8, yl + 2 * FH
    gy = lax.axis_index("gy")
    src_l = src[0]
    own, halo = pl.ds(0, xl), pl.ds(xl, 8)

    def put(name, c, row, cols, value):
        if name == "co":
            cx[row, cols, :] = value
        else:
            (e0 if name == "fe" else h)[c, row, cols, :] = value

    to = Halo(mon[0], xl, yl, put)
    fill_own((fe, fh), (e0, h), xl, yl)
    for y in range(yl):
        cx[FH + y, own, :] = co[y]
    names = FWD + ("co",)
    raw, win = x_parts(yl)
    to.tiles(rx, raw, win, names, lambda y: FH + y)
    at_src = lax.broadcasted_iota(jnp.int32, (xl, 128), 1) == src_l
    at_src8 = lax.broadcasted_iota(jnp.int32, (8, 128), 1) == src_l

    def source(row, wide, tile, lane):
        sx[row, own, :] = jnp.where(at_src, jnp.broadcast_to(wide[:, lane : lane + 1], (xl, 128)), 0.0)
        sx[row, halo, :] = jnp.where(at_src8, jnp.broadcast_to(tile[:, lane : lane + 1], (8, 128)), 0.0)

    prof, prof_x = prof_t[...], rx[rx.shape[0] - 1] * to.keep
    for y in range(yl):
        source(FH + y, prof, prof_x, y)
    for ref, ref_d, high in ((ra, rda, gy % 2 == 0), (rb, rdb, gy % 2 == 1)):
        to.side(ref, F_RAW, F_WIN, high)
        to.tiles(ref_d, C_RAW, C_WIN, names, lambda i, high=high: to.row(i, high))
        prof_y, prof_d = ref[ref.shape[0] - 1], ref_d[ref_d.shape[0] - 1] * to.keep
        for i in range(FH):
            source(to.row(i, high), prof_y, prof_d, PROF + i)
    step = Stepper(xl, yl, cx)
    runs = (e0, e1, e2, e3)
    for k in range(STEPS):
        new = runs[k + 1]
        signal = pick([s[k] for s in signals])
        for y, cur, inc in step.rows(runs[k], h, k, yr - 1 - k):
            new[0, y] = cur[0] + inc[0] + signal * sx[y]
            new[1, y] = cur[1] + inc[1]
            new[2, y] = cur[2] + inc[2]
    put_out(e3, out, xl, yl)


def adjoint_body(mon, ae, ah, cx, e1, e2, e3, ra, rb, rx, rda, rdb, out, grad, a, g, *, xl, yl, omegas):
    yr = yl + 2 * FH
    gy = lax.axis_index("gy")

    def put(name, c, row, cols, value):
        (a if name == "ae" else g)[c, row, cols, :] = value

    to = Halo(mon[0], xl, yl, put)
    fill_own((ae, ah), (a, g), xl, yl)
    raw, win = x_parts(yl)
    to.tiles(rx, raw, win, ADJ, lambda y: FH + y)
    for ref, ref_d, high in ((ra, rda, gy % 2 == 0), (rb, rdb, gy % 2 == 1)):
        to.side(ref, A_RAW, [], high)
        to.tiles(ref_d, C_RAW, C_WIN, ADJ, lambda i, high=high: to.row(i, high))
    step = Stepper(xl, yl, cx)
    at_mon = step.lane == mon[0]
    total = [None] * yl
    for j in range(STEPS):
        seen = (e3, e2, e1)[j]
        for y, cur, inc in step.rows(a, g, FH - AH + j, yr - AH - j):
            for c in range(3):
                f = seen[c, y]
                v = cur[c] + inc[c] + jnp.where(at_mon, 2.0 * DT * f, 0.0)
                a[c, y] = v
                if FH <= y < FH + yl:
                    t = (f * v)[0:xl]
                    i = y - FH
                    total[i] = t if total[i] is None else total[i] + t
    scale = pick([o * o for o in omegas])
    lane = step.lane[0:xl]
    packed = jnp.zeros((xl, 128), F32)
    wide = 128 // yl
    for y in range(yl):
        moved = pltpu.roll(total[y] * scale, (wide * y - Z0) % 128, 1)
        packed = jnp.where((lane >= wide * y) & (lane < wide * (y + 1)), moved, packed)
    grad[...] = packed
    put_out(a, out, xl, yl)


def sum_body(*refs, owned, xl, yl):
    *parts, out, turn = refs
    w = lax.axis_index("wl")
    acc = parts[0][...]
    for p in parts[1:]:
        acc = acc + p[...]
    turn[...] = jnp.transpose(acc)
    for i in range(owned):
        out[i] = turn[pl.ds(owned * w + i, yl, stride=128 // yl), :]


def per_device(fe, fh, ae, ah, background, design, source_profile, source_layer, monitor_layer):
    _, _, xl, yl, nz = fe.shape
    nw = lax.axis_size("wl")
    owned = design.shape[0]
    xr, yr = xl + 8, yl + 2 * FH
    flat = [v.reshape(3 * xl * yl, nz) for v in (fe, fh, ae, ah)] + [background.reshape(xl * yl, nz)]
    sp = jnp.transpose(source_profile[0])
    shape = lambda *s: jax.ShapeDtypeStruct(s, F32)
    smem = pl.BlockSpec(memory_space=pltpu.SMEM)
    vmem = pl.BlockSpec(memory_space=pltpu.VMEM)
    hbm = pl.BlockSpec(memory_space=pltpu.HBM)
    ext = lambda *s: pltpu.VMEM(s, F32)
    field = (3, yr, xr, nz)

    def call(body, name, out, specs, scratch=()):
        return pl.pallas_call(
            body, out_shape=tuple(shape(*s) for s in out), in_specs=specs, out_specs=(vmem,) * len(out),
            scratch_shapes=list(scratch), name=name,
            compiler_params=pltpu.CompilerParams(vmem_limit_bytes=20 * 1024 * 1024),
        )

    def over_wl(v):
        return [v] + [lax.ppermute(v, "wl", [(i, i ^ k) for i in range(nw)]) for k in range(1, nw)]

    raw, win = x_parts(yl)
    f_side = (len(F_RAW) + ceil(len(F_WIN), PER), xl, nz)
    a_side = (len(A_RAW), xl, nz)
    corner = (ceil(len(C_RAW), 2) + ceil(len(C_WIN), PER), 8, nz)
    beside = (ceil(len(raw), 2) + ceil(len(win), PER) + 1, 8, nz)

    layers = over_wl(jnp.transpose(design, (0, 2, 1)))
    held = call(fetch_body, "fetch", [v.shape for v in flat], [hbm] * 5, [pltpu.SemaphoreType.DMA((5,))])(
        *[pltpu.with_memory_space_constraint(v, pltpu.HBM) for v in flat])
    co, prof_t, fa, fb, aa, ab, px, da, db = call(
        lambda *r: send_body(*r, xl=xl, yl=yl, nw=nw, owned=owned), "send",
        [(yl, xl, nz), (xl, nz), f_side, f_side, a_side, a_side, beside, corner, corner],
        [smem] + [vmem] * (6 + nw), [ext(128, 128)],
    )(monitor_layer, *held, sp, *layers)
    rfa, rfb = swap(fa, False, 0), swap(fb, False, 1)
    rx = swap(px, True, None)
    rda, rdb = swap(da, True, 0), swap(db, True, 1)
    raa, rab = swap(aa, False, 0), swap(ab, False, 1)
    f32 = np.float32
    omegas = [f32(2.0 * math.pi) / (f32(16.0) + f32(32.0) * f32(i) / f32(nw)) for i in range(nw)]
    signals = [[f32(DT) * np.sin(f32(o * f32((k + 1) * DT))) for k in range(STEPS)] for o in omegas]
    out_f, cx, e1, e2, e3 = call(
        lambda *r: forward_body(*r, xl=xl, yl=yl, signals=signals), "forward",
        [flat[0].shape, (yr, xr, nz), field, field, field], [smem, smem] + [vmem] * 9,
        [ext(*field), ext(*field), ext(yr, xr, nz)],
    )(source_layer, monitor_layer, held[0], held[1], co, prof_t, rfa, rfb, rx, rda, rdb)
    out_a, grad = call(
        lambda *r: adjoint_body(*r, xl=xl, yl=yl, omegas=omegas), "adjoint",
        [flat[0].shape, (xl, nz)], [smem] + [vmem] * 11, [ext(*field), ext(*field)],
    )(monitor_layer, held[2], held[3], cx, e1, e2, e3, raa, rab, rx, rda, rdb)
    (gradient,) = call(
        lambda *r: sum_body(*r, owned=owned, xl=xl, yl=yl), "gather_sum",
        [(owned, yl, xl)], [vmem] * nw, [ext(128, xl)],
    )(*over_wl(grad))
    block = (1, 3, xl, yl, nz)
    return (out_f.reshape(block), out_a.reshape(block), jnp.transpose(gradient, (0, 2, 1)))


def solution(mesh):
    field = P("wl", None, "gx", "gy", None)
    return jax.shard_map(
        per_device,
        mesh=mesh,
        in_specs=(field, field, field, field, P("gx", "gy", None), P("wl", "gx", "gy"),
                  P("wl", "gx", "gy"), P("wl"), P("wl")),
        out_specs=(field, field, P("wl", "gx", "gy")),
        check_vma=False,
    )
```

```python
import math

import jax
import jax.numpy as jnp
import numpy as np
from jax import lax
from jax.experimental import pallas as pl
from jax.experimental.pallas import tpu as pltpu
from jax.sharding import PartitionSpec as P

Z0 = 64
STEPS = 3
DT = 0.5
F32 = jnp.float32
BF16 = jnp.bfloat16
FH = 5
AH = 3
WIN = 16
PER = 128 // WIN
PROF = 112


def swap(block, flip_x, parity):
    nx, ny = lax.axis_size("gx"), lax.axis_size("gy")
    route = []
    for a in range(nx):
        for b in range(ny):
            ta = a ^ 1 if flip_x else a
            tb = b if parity is None else ((b + parity) ^ 1) - parity
            if 0 <= ta < nx and 0 <= tb < ny:
                route.append((a * ny + b, ta * ny + tb))
    return lax.ppermute(block, ("gx", "gy"), route)


FWD, ADJ = ("fe", "fh"), ("ae", "ah")
def side_parts(e, h):
    return [(e, c, i) for c in range(3) for i in range(2)] + [(h, c, i) for c in range(3) for i in range(2)] + [(h, 0, 2), (h, 2, 2)]


CO_RAW, CO_WIN = [("co", 0, i) for i in (0, 1)], [("co", 0, i) for i in (2, 3)]
F_RAW = side_parts(*FWD) + CO_RAW
A_RAW = side_parts(*ADJ)
F_WIN = [("fe", c, i) for c in range(3) for i in (2, 3, 4)] + [("fh", 1, 2)]
F_WIN += [("fh", c, i) for c in range(3) for i in (3, 4)] + CO_WIN
C_RAW = side_parts(*FWD) + [("fe", 1, 2)] + A_RAW + [("ae", 1, 2)] + CO_RAW
C_WIN = [(n, c, i) for n in FWD for c in range(3) for i in range(FH)] + CO_RAW + CO_WIN


def x_parts(yl):
    raw = [(n, c, y) for n in FWD + ADJ for c in range(3) for y in range(yl)]
    win = [(n, c, y) for n in FWD for c in range(3) for y in range(yl)]
    co = [("co", 0, y) for y in range(yl)]
    return raw + co, win + co


def ceil(a, b):
    return -(-a // b)


def stepped(e, h, out, xl, yl):
    sub = lax.broadcasted_iota(jnp.int32, (xl, 128), 0)
    x_last = sub == xl - 1
    z_last = lax.broadcasted_iota(jnp.int32, (xl, 128), 1) == 127
    zup = lambda v: jnp.where(z_last, 0.0, pltpu.roll(v, 127, 1)) - v
    xup = lambda v: jnp.where(x_last, 0.0, pltpu.roll(v, xl - 1, 0)) - v
    row = lambda ref, c, y: ref[pl.ds(c * xl * yl + y, xl, stride=yl), :]
    cur = [row(e, c, 0) for c in range(3)]
    for y in range(yl - 1):
        up = [row(e, c, y + 1) for c in range(3)]
        ex, ey, ez = cur
        out[0, y] = row(h, 0, y) - DT * ((up[2] - ez) - zup(ey))
        out[1, y] = row(h, 1, y) - DT * (zup(ex) - xup(ez))
        out[2, y] = row(h, 2, y) - DT * (xup(ey) - (up[0] - ex))
        cur = up


def edge_row(e, h, h1, is_h, c, i, up, x, count, xl, yl):
    here = jnp.where(up, yl - 1 - i, i)
    flat = lambda ref, r: ref[pl.ds(c * xl * yl + x * yl + r, count, stride=yl), :]
    if not is_h:
        return flat(e, here)
    if i in (1, 2):
        return h1[c, here, pl.ds(x, count), :]
    return jnp.where(up, flat(h, yl - 1 - i), h1[c, i, pl.ds(x, count), :])


def fetch_body(ae, ah, fe, fh, bg, *rest, xl, yl):
    outs, (h1, aa, ab, sems) = rest[:5], rest[5:]
    copies = [pltpu.make_async_copy(s, d, sems.at[i]) for i, (s, d) in enumerate(zip((ae, ah, fe, fh, bg), outs))]
    for c in copies:
        c.start()
    copies[0].wait()
    copies[1].wait()
    e, h = outs[0], outs[1]
    gy = lax.axis_index("gy")
    stepped(e, h, h1, xl, yl)
    for u, (name, c, i) in enumerate(A_RAW):
        for dst, up in ((aa, gy % 2 == 0), (ab, gy % 2 == 1)):
            dst[u] = edge_row(e, h, h1, name == "ah", c, i, up, 0, xl, xl, yl)
    for c in copies[2:]:
        c.wait()


def first_body(fe, fh, h1, *, xl, yl):
    stepped(fe, fh, h1, xl, yl)


def send_body(mon, fe, fh, ae, ah, bg, fh1, ah1, sp, *rest, xl, yl, nw, owned):
    parts, (co, prof_t, fa, fb, px, da, db, turn) = rest[:nw], rest[nw:]
    gx, gy, w = lax.axis_index("gx"), lax.axis_index("gy"), lax.axis_index("wl")
    plane = xl * yl
    depth = nw * owned
    lane = lax.broadcasted_iota(jnp.int32, (xl, 128), 1)
    lane8 = lane[0:8]
    first = WIN // 2 - mon[0] + 256
    refs = dict(fe=fe, fh=fh, ae=ae, ah=ah)
    turn[...] = jnp.zeros((128, 128), F32)
    for k in range(nw):
        for i in range(owned):
            turn[pl.ds(owned * (w ^ k) + i, yl, stride=depth), 0:xl] = parts[k][i]
    layers = jnp.transpose(turn[...])[0:xl]
    for y in range(yl):
        moved = pltpu.roll(layers, (Z0 - depth * y) % 128, 1)
        perm = jnp.where((lane >= Z0) & (lane < Z0 + depth), moved, bg[pl.ds(y, xl, stride=yl), :])
        co[y] = DT / perm
    turn[0:yl, 0:xl] = sp[...]
    prof_t[...] = jnp.transpose(turn[...])[0:xl]
    low_x = gx == 0
    x8 = pl.multiple_of(jnp.where(low_x, xl - 8, 0), 8)

    def beside(name, c, y, x, count):
        if name == "co":
            return co[y, pl.ds(x, count), :]
        return refs[name][pl.ds(c * plane + x * yl + y, count, stride=yl), :]

    def beyond(up):
        def rows(name, c, i, x, count):
            if name == "co":
                return co[jnp.where(up, yl - 1 - i, i), pl.ds(x, count), :]
            e, h, h1 = (fe, fh, fh1) if name in FWD else (ae, ah, ah1)
            return edge_row(e, h, h1, name in ("fh", "ah"), c, i, up, x, count, xl, yl)
        return rows

    def windows(parts, x, count, rows):
        out = []
        here = lax.broadcasted_iota(jnp.int32, (count, 128), 1)
        for t in range(ceil(len(parts), PER)):
            acc = jnp.zeros((count, 128), F32)
            for q, (name, c, i) in enumerate(parts[t * PER : (t + 1) * PER]):
                moved = pltpu.roll(rows(name, c, i, x, count), (WIN * q + first) % 128, 1)
                acc = jnp.where((here >= WIN * q) & (here < WIN * (q + 1)), moved, acc)
            out.append(acc)
        return out

    def tiles(dst, raw, win, rows):
        for n, (name, c, i) in enumerate(raw):
            half = pltpu.roll(rows(name, c, i, x8, 8), jnp.where(low_x, 4, 0), 0)[0:4]
            dst[n // 2, 4 * (n % 2) : 4 * (n % 2) + 4, :] = half
        at = ceil(len(raw), 2)
        for tile in windows(win, x8, 8, rows):
            dst[at] = tile
            at += 1
        return at

    for dst, corner, up in ((fa, da, gy % 2 == 0), (fb, db, gy % 2 == 1)):
        rows = beyond(up)
        for u, (name, c, i) in enumerate(F_RAW):
            dst[u] = rows(name, c, i, 0, xl)
        at = len(F_RAW)
        for unit in windows(F_WIN, 0, xl, rows):
            dst[at] = unit
            at += 1
        mix = dst[at - 1]
        prof = prof_t[...]
        for i in range(FH):
            col = jnp.where(up, prof[:, yl - 1 - i : yl - i], prof[:, i : i + 1])
            mix = jnp.where(lane == PROF + i, jnp.broadcast_to(col, (xl, 128)), mix)
        dst[at - 1] = mix
        last = tiles(corner, C_RAW, C_WIN, rows)
        src8 = dst[at - 1, pl.ds(x8, 8), :]
        corner[last - 1] = jnp.where((lane8 >= PROF) & (lane8 < PROF + FH), src8, corner[last - 1])
    raw, win = x_parts(yl)
    last = tiles(px, raw, win, beside)
    px[last] = prof_t[pl.ds(x8, 8), :]


class Halo:
    def __init__(self, mon, xl, yl, put):
        self.xl, self.yl, self.put = xl, yl, put
        self.gx, self.gy = lax.axis_index("gx"), lax.axis_index("gy")
        self.back = mon - WIN // 2 + 256
        sub = lax.broadcasted_iota(jnp.int32, (8, 128), 0)
        low = self.gx == 0
        mask = lambda lo, hi: jnp.where(low, lo.astype(F32), hi.astype(F32))
        self.keep = mask(sub < FH, sub >= 8 - FH)
        self.near = mask(sub < 4, sub >= 4) > 0.5
        self.far = mask((sub >= 4) & (sub < FH), (sub < 4) & (sub >= 8 - FH)) > 0.5
        self.shift = [jnp.where(low, 0, 4), jnp.where(low, 4, 0)]

    def row(self, i, high):
        return jnp.where(high, FH + self.yl + i, FH - 1 - i)

    def unroll(self, tile, q):
        return pltpu.roll(tile, (self.back - WIN * q) % 128, 1)

    def side(self, ref, raw, win, high):
        own = pl.ds(0, self.xl)
        for u, (name, c, i) in enumerate(raw):
            self.put(name, c, self.row(i, high), own, ref[u])
        for s, (name, c, i) in enumerate(win):
            self.put(name, c, self.row(i, high), own, self.unroll(ref[len(raw) + s // PER], s % PER))

    def tiles(self, ref, raw, win, names, where):
        halo = pl.ds(self.xl, 8)
        seats = {part: s for s, part in enumerate(win)}
        at = ceil(len(raw), 2)
        for n, part in enumerate(raw):
            if part[0] not in names:
                continue
            value = jnp.where(self.near, pltpu.roll(ref[n // 2], self.shift[n % 2], 0), 0.0)
            if part in seats:
                s = seats.pop(part)
                value = jnp.where(self.far, self.unroll(ref[at + s // PER], s % PER), value)
            self.put(part[0], part[1], where(part[2]), halo, value)
        for part, s in seats.items():
            if part[0] in names:
                self.put(part[0], part[1], where(part[2]), halo, self.unroll(ref[at + s // PER], s % PER) * self.keep)


class Stepper:
    def __init__(self, xl, yl, cx):
        self.xr = xr = xl + 8
        self.cx = cx
        gx, gy = lax.axis_index("gx"), lax.axis_index("gy")
        self.lane = lax.broadcasted_iota(jnp.int32, (xr, 128), 1)
        ring = lax.broadcasted_iota(jnp.int32, (xr, 128), 0)
        inside_low = jnp.where(ring < xl + FH, F32(DT), F32(0.0))
        inside_high = jnp.where((ring < xl) | (ring >= xr - FH), F32(DT), F32(0.0))
        self.h_in = jnp.where(gx == 0, inside_low, inside_high)
        self.h_low = self.h_in * jnp.where(gy == 0, 0.0, 1.0).astype(F32)
        edge = ((ring == xl - 1) | (ring == xr - 1)).astype(F32)
        self.h_edge = self.h_in * edge
        self.z_last = self.lane == 127
        ri = lax.broadcasted_iota(jnp.int32, (128, 128), 0)
        ci = lax.broadcasted_iota(jnp.int32, (128, 128), 1)
        diff = jnp.where(ri == ci, F32(1.0), F32(0.0)) - jnp.where(ri == ci - 1, F32(1.0), F32(0.0))
        self.diff = jnp.concatenate([diff] * 3, 0).astype(BF16)

    def zdn(self, p, q):
        v = jnp.concatenate([p, q], 0)
        hi = v.astype(BF16)
        rest = v - hi.astype(F32)
        mid = rest.astype(BF16)
        low = (rest - mid.astype(F32)).astype(BF16)
        out = lax.dot_general(jnp.concatenate([hi, mid, low], 1), self.diff, (((1,), (0,)), ((), ())),
                              preferred_element_type=F32)
        return out[0 : self.xr], out[self.xr :]

    def zup(self, v):
        return jnp.where(self.z_last, 0.0, pltpu.roll(v, 127, 1)) - v

    def xup(self, v):
        return pltpu.roll(v, self.xr - 1, 0) - v

    def xdn(self, v):
        return v - pltpu.roll(v, 1, 0)

    def rows(self, e, h, start, stop, given=()):
        load = lambda ref, y: (ref[0, y], ref[1, y], ref[2, y])
        cur, now = load(e, start), None
        for y in range(start, stop):
            up = load(e, y + 1)
            below = now
            k = self.h_low if y < FH else self.h_in
            ex, ey, ez = cur
            if y in given:
                k = self.h_edge
                now = (
                    h[0, y],
                    h[1, y] + k * pltpu.roll(ez, self.xr - 1, 0),
                    h[2, y] - k * pltpu.roll(ey, self.xr - 1, 0),
                )
            else:
                now = (
                    h[0, y] - k * ((up[2] - ez) - self.zup(ey)),
                    h[1, y] - k * (self.zup(ex) - self.xup(ez)),
                    h[2, y] - k * (self.xup(ey) - (up[0] - ex)),
                )
            for c in range(3):
                h[c, y] = now[c]
            if y > start:
                hx, hy, hz = now
                k = self.cx[y]
                zy, zx = self.zdn(hy, hx)
                yield y, cur, (
                    k * ((hz - below[2]) - zy),
                    k * (zx - self.xdn(hz)),
                    k * (self.xdn(hy) - (hx - below[0])),
                )
            cur = up


def given_rows(yl):
    return {FH - 3, FH - 2, *range(FH + yl, yl + 2 * FH)}


def pick(values):
    w = lax.axis_index("wl")
    value = F32(values[0])
    for i in range(1, len(values)):
        value = jnp.where(w == i, F32(values[i]), value)
    return value


def fill_own(refs, bigs, xl, yl):
    for ref, big in zip(refs, bigs):
        for c in range(3):
            for y in range(yl):
                big[c, FH + y, 0:xl, :] = ref[pl.ds(c * xl * yl + y, xl, stride=yl), :]


def put_out(big, out, xl, yl):
    for c in range(3):
        for y in range(yl):
            out[pl.ds(c * xl * yl + y, xl, stride=yl), :] = big[c, FH + y, 0:xl, :]


def forward_body(src, mon, fe, fh, co, prof_t, ra, rb, rx, rda, rdb, out, cx, e1, e2, e3, e0, h, sx, *, xl, yl, signals):
    xr, yr = xl + 8, yl + 2 * FH
    gy = lax.axis_index("gy")
    src_l = src[0]
    own, halo = pl.ds(0, xl), pl.ds(xl, 8)

    def put(name, c, row, cols, value):
        if name == "co":
            cx[row, cols, :] = value
        else:
            (e0 if name == "fe" else h)[c, row, cols, :] = value

    to = Halo(mon[0], xl, yl, put)
    fill_own((fe, fh), (e0, h), xl, yl)
    for y in range(yl):
        cx[FH + y, own, :] = co[y]
    names = FWD + ("co",)
    raw, win = x_parts(yl)
    to.tiles(rx, raw, win, names, lambda y: FH + y)
    at_src = lax.broadcasted_iota(jnp.int32, (xl, 128), 1) == src_l
    at_src8 = lax.broadcasted_iota(jnp.int32, (8, 128), 1) == src_l

    def source(row, wide, tile, lane):
        sx[row, own, :] = jnp.where(at_src, jnp.broadcast_to(wide[:, lane : lane + 1], (xl, 128)), 0.0)
        sx[row, halo, :] = jnp.where(at_src8, jnp.broadcast_to(tile[:, lane : lane + 1], (8, 128)), 0.0)

    prof, prof_x = prof_t[...], rx[rx.shape[0] - 1] * to.keep
    for y in range(yl):
        source(FH + y, prof, prof_x, y)
    for ref, ref_d, high in ((ra, rda, gy % 2 == 0), (rb, rdb, gy % 2 == 1)):
        to.side(ref, F_RAW, F_WIN, high)
        to.tiles(ref_d, C_RAW, C_WIN, names, lambda i, high=high: to.row(i, high))
        prof_y, prof_d = ref[ref.shape[0] - 1], ref_d[ref_d.shape[0] - 1] * to.keep
        for i in range(FH):
            source(to.row(i, high), prof_y, prof_d, PROF + i)
    step = Stepper(xl, yl, cx)
    runs = (e0, e1, e2, e3)
    for k in range(STEPS):
        new = runs[k + 1]
        signal = pick([s[k] for s in signals])
        for y, cur, inc in step.rows(runs[k], h, k, yr - 1 - k, given_rows(yl) if k == 0 else ()):
            new[0, y] = cur[0] + inc[0] + signal * sx[y]
            new[1, y] = cur[1] + inc[1]
            new[2, y] = cur[2] + inc[2]
    put_out(e3, out, xl, yl)


def adjoint_body(mon, ae, ah, cx, e1, e2, e3, ra, rb, rx, rda, rdb, out, grad, a, g, *, xl, yl, omegas):
    yr = yl + 2 * FH
    gy = lax.axis_index("gy")

    def put(name, c, row, cols, value):
        (a if name == "ae" else g)[c, row, cols, :] = value

    to = Halo(mon[0], xl, yl, put)
    for c in range(3):
        a[c, FH - AH] = jnp.zeros((xl + 8, 128), F32)
    fill_own((ae, ah), (a, g), xl, yl)
    raw, win = x_parts(yl)
    to.tiles(rx, raw, win, ADJ, lambda y: FH + y)
    for ref, ref_d, high in ((ra, rda, gy % 2 == 0), (rb, rdb, gy % 2 == 1)):
        to.side(ref, A_RAW, [], high)
        to.tiles(ref_d, C_RAW, C_WIN, ADJ, lambda i, high=high: to.row(i, high))
    step = Stepper(xl, yl, cx)
    at_mon = step.lane == mon[0]
    total = [None] * yl
    for j in range(STEPS):
        seen = (e3, e2, e1)[j]
        for y, cur, inc in step.rows(a, g, FH - AH + j, yr - AH - j, given_rows(yl) if j == 0 else ()):
            for c in range(3):
                f = seen[c, y]
                v = cur[c] + inc[c] + jnp.where(at_mon, 2.0 * DT * f, 0.0)
                a[c, y] = v
                if FH <= y < FH + yl:
                    t = (f * v)[0:xl]
                    i = y - FH
                    total[i] = t if total[i] is None else total[i] + t
    scale = pick([o * o for o in omegas])
    lane = step.lane[0:xl]
    packed = jnp.zeros((xl, 128), F32)
    wide = 128 // yl
    for y in range(yl):
        moved = pltpu.roll(total[y] * scale, (wide * y - Z0) % 128, 1)
        packed = jnp.where((lane >= wide * y) & (lane < wide * (y + 1)), moved, packed)
    grad[...] = packed
    put_out(a, out, xl, yl)


def sum_body(*refs, owned, xl, yl):
    *parts, out, turn = refs
    w = lax.axis_index("wl")
    acc = parts[0][...]
    for p in parts[1:]:
        acc = acc + p[...]
    turn[...] = jnp.transpose(acc)
    for i in range(owned):
        out[i] = turn[pl.ds(owned * w + i, yl, stride=128 // yl), :]


def per_device(fe, fh, ae, ah, background, design, source_profile, source_layer, monitor_layer):
    _, _, xl, yl, nz = fe.shape
    nw = lax.axis_size("wl")
    owned = design.shape[0]
    xr, yr = xl + 8, yl + 2 * FH
    flat = [v.reshape(3 * xl * yl, nz) for v in (fe, fh, ae, ah)] + [background.reshape(xl * yl, nz)]
    sp = jnp.transpose(source_profile[0])
    shape = lambda *s: jax.ShapeDtypeStruct(s, F32)
    smem = pl.BlockSpec(memory_space=pltpu.SMEM)
    vmem = pl.BlockSpec(memory_space=pltpu.VMEM)
    hbm = pl.BlockSpec(memory_space=pltpu.HBM)
    ext = lambda *s: pltpu.VMEM(s, F32)
    field = (3, yr, xr, nz)

    def call(body, name, out, specs, scratch=()):
        return pl.pallas_call(
            body, out_shape=tuple(shape(*s) for s in out), in_specs=specs, out_specs=(vmem,) * len(out),
            scratch_shapes=list(scratch), name=name,
            compiler_params=pltpu.CompilerParams(vmem_limit_bytes=20 * 1024 * 1024),
        )

    def over_wl(v):
        return [v] + [lax.ppermute(v, "wl", [(i, i ^ k) for i in range(nw)]) for k in range(1, nw)]

    raw, win = x_parts(yl)
    f_side = (len(F_RAW) + ceil(len(F_WIN), PER), xl, nz)
    a_side = (len(A_RAW), xl, nz)
    corner = (ceil(len(C_RAW), 2) + ceil(len(C_WIN), PER), 8, nz)
    beside = (ceil(len(raw), 2) + ceil(len(win), PER) + 1, 8, nz)

    layers = over_wl(jnp.transpose(design, (0, 2, 1)))
    fe, fh, ae, ah, bg = flat
    h1 = (3, yl, xl, nz)
    ae, ah, fe, fh, bg, ah1, aa, ab = call(
        lambda *r: fetch_body(*r, xl=xl, yl=yl), "fetch",
        [ae.shape] * 4 + [bg.shape, h1, a_side, a_side], [hbm] * 5, [pltpu.SemaphoreType.DMA((5,))],
    )(*[pltpu.with_memory_space_constraint(v, pltpu.HBM) for v in (ae, ah, fe, fh, bg)])
    raa, rab = swap(aa, False, 0), swap(ab, False, 1)
    (fh1,) = call(lambda *r: first_body(*r, xl=xl, yl=yl), "first", [h1], [vmem] * 2)(fe, fh)
    co, prof_t, fa, fb, px, da, db = call(
        lambda *r: send_body(*r, xl=xl, yl=yl, nw=nw, owned=owned), "send",
        [(yl, xl, nz), (xl, nz), f_side, f_side, beside, corner, corner],
        [smem] + [vmem] * (8 + nw), [ext(128, 128)],
    )(monitor_layer, fe, fh, ae, ah, bg, fh1, ah1, sp, *layers)
    rfa, rfb = swap(fa, False, 0), swap(fb, False, 1)
    rx = swap(px, True, None)
    rda, rdb = swap(da, True, 0), swap(db, True, 1)
    f32 = np.float32
    omegas = [f32(2.0 * math.pi) / (f32(16.0) + f32(32.0) * f32(i) / f32(nw)) for i in range(nw)]
    signals = [[f32(DT) * np.sin(f32(o * f32((k + 1) * DT))) for k in range(STEPS)] for o in omegas]
    out_f, cx, e1, e2, e3 = call(
        lambda *r: forward_body(*r, xl=xl, yl=yl, signals=signals), "forward",
        [flat[0].shape, (yr, xr, nz), field, field, field], [smem, smem] + [vmem] * 9,
        [ext(*field), ext(*field), ext(yr, xr, nz)],
    )(source_layer, monitor_layer, fe, fh, co, prof_t, rfa, rfb, rx, rda, rdb)
    out_a, grad = call(
        lambda *r: adjoint_body(*r, xl=xl, yl=yl, omegas=omegas), "adjoint",
        [flat[0].shape, (xl, nz)], [smem] + [vmem] * 11, [ext(*field), ext(*field)],
    )(monitor_layer, ae, ah, cx, e1, e2, e3, raa, rab, rx, rda, rdb)
    (gradient,) = call(
        lambda *r: sum_body(*r, owned=owned, xl=xl, yl=yl), "gather_sum",
        [(owned, yl, xl)], [vmem] * nw, [ext(128, xl)],
    )(*over_wl(grad))
    block = (1, 3, xl, yl, nz)
    return (out_f.reshape(block), out_a.reshape(block), jnp.transpose(gradient, (0, 2, 1)))


def solution(mesh):
    field = P("wl", None, "gx", "gy", None)
    return jax.shard_map(
        per_device,
        mesh=mesh,
        in_specs=(field, field, field, field, P("gx", "gy", None), P("wl", "gx", "gy"),
                  P("wl", "gx", "gy"), P("wl"), P("wl")),
        out_specs=(field, field, P("wl", "gx", "gy")),
        check_vma=False,
    )
```

```python
import math

import jax
import jax.numpy as jnp
import numpy as np
from jax import lax
from jax.experimental import pallas as pl
from jax.experimental.pallas import tpu as pltpu
from jax.sharding import PartitionSpec as P

Z0 = 64
STEPS = 3
DT = 0.5
F32 = jnp.float32
BF16 = jnp.bfloat16
FH = 5
AH = 3
WIN = 16
PER = 128 // WIN
PROF = 112


def swap(block, flip_x, parity):
    nx, ny = lax.axis_size("gx"), lax.axis_size("gy")
    route = []
    for a in range(nx):
        for b in range(ny):
            ta = a ^ 1 if flip_x else a
            tb = b if parity is None else ((b + parity) ^ 1) - parity
            if 0 <= ta < nx and 0 <= tb < ny:
                route.append((a * ny + b, ta * ny + tb))
    return lax.ppermute(block, ("gx", "gy"), route)


FWD, ADJ = ("fe", "fh"), ("ae", "ah")
def side_parts(e, h):
    return [(e, c, i) for c in range(3) for i in range(2)] + [(h, c, i) for c in range(3) for i in range(2)] + [(h, 0, 2), (h, 2, 2)]


CO_RAW, CO_WIN = [("co", 0, i) for i in (0, 1)], [("co", 0, i) for i in (2, 3)]
F_RAW = side_parts(*FWD) + CO_RAW
A_RAW = side_parts(*ADJ)
F_WIN = [("fe", c, i) for c in range(3) for i in (2, 3, 4)] + [("fh", 1, 2)]
F_WIN += [("fh", c, i) for c in range(3) for i in (3, 4)] + CO_WIN
C_RAW = side_parts(*FWD) + [("fe", 1, 2)] + A_RAW + [("ae", 1, 2)] + CO_RAW
C_WIN = [(n, c, i) for n in FWD for c in range(3) for i in range(FH)] + CO_RAW + CO_WIN


def x_parts(yl):
    raw = [(n, c, y) for n in FWD + ADJ for c in range(3) for y in range(yl)]
    win = [(n, c, y) for n in FWD for c in range(3) for y in range(yl)]
    co = [("co", 0, y) for y in range(yl)]
    return raw + co, win + co


def ceil(a, b):
    return -(-a // b)


def stepped(e, h, out, xl, yl):
    sub = lax.broadcasted_iota(jnp.int32, (xl, 128), 0)
    x_last = sub == xl - 1
    z_last = lax.broadcasted_iota(jnp.int32, (xl, 128), 1) == 127
    zup = lambda v: jnp.where(z_last, 0.0, pltpu.roll(v, 127, 1)) - v
    xup = lambda v: jnp.where(x_last, 0.0, pltpu.roll(v, xl - 1, 0)) - v
    row = lambda ref, c, y: ref[pl.ds(c * xl * yl + y, xl, stride=yl), :]
    cur = [row(e, c, 0) for c in range(3)]
    for y in range(yl - 1):
        up = [row(e, c, y + 1) for c in range(3)]
        ex, ey, ez = cur
        out[0, y] = row(h, 0, y) - DT * ((up[2] - ez) - zup(ey))
        out[1, y] = row(h, 1, y) - DT * (zup(ex) - xup(ez))
        out[2, y] = row(h, 2, y) - DT * (xup(ey) - (up[0] - ex))
        cur = up


def edge_row(e, h, h1, is_h, c, i, up, x, count, xl, yl):
    here = jnp.where(up, yl - 1 - i, i)
    flat = lambda ref, r: ref[pl.ds(c * xl * yl + x * yl + r, count, stride=yl), :]
    if not is_h:
        return flat(e, here)
    if i in (1, 2):
        return h1[c, here, pl.ds(x, count), :]
    return jnp.where(up, flat(h, yl - 1 - i), h1[c, i, pl.ds(x, count), :])


def fetch_body(ae, ah, fe, fh, bg, *rest, xl, yl):
    outs, (h1, aa, ab, sems) = rest[:5], rest[5:]
    copies = [pltpu.make_async_copy(s, d, sems.at[i]) for i, (s, d) in enumerate(zip((ae, ah, fe, fh, bg), outs))]
    for c in copies:
        c.start()
    copies[0].wait()
    copies[1].wait()
    e, h = outs[0], outs[1]
    gy = lax.axis_index("gy")
    stepped(e, h, h1, xl, yl)
    for u, (name, c, i) in enumerate(A_RAW):
        for dst, up in ((aa, gy % 2 == 0), (ab, gy % 2 == 1)):
            dst[u] = edge_row(e, h, h1, name == "ah", c, i, up, 0, xl, xl, yl)
    for c in copies[2:]:
        c.wait()


def first_body(fe, fh, h1, *, xl, yl):
    stepped(fe, fh, h1, xl, yl)


def send_body(mon, fe, fh, ae, ah, bg, fh1, ah1, sp, *rest, xl, yl, nw, owned):
    parts, (co, prof_t, fa, fb, px, da, db, turn) = rest[:nw], rest[nw:]
    gx, gy, w = lax.axis_index("gx"), lax.axis_index("gy"), lax.axis_index("wl")
    plane = xl * yl
    depth = nw * owned
    lane = lax.broadcasted_iota(jnp.int32, (xl, 128), 1)
    lane8 = lane[0:8]
    first = WIN // 2 - mon[0] + 256
    refs = dict(fe=fe, fh=fh, ae=ae, ah=ah)
    turn[...] = jnp.zeros((128, 128), F32)
    for k in range(nw):
        for i in range(owned):
            turn[pl.ds(owned * (w ^ k) + i, yl, stride=depth), 0:xl] = parts[k][i]
    layers = jnp.transpose(turn[...])[0:xl]
    for y in range(yl):
        moved = pltpu.roll(layers, (Z0 - depth * y) % 128, 1)
        perm = jnp.where((lane >= Z0) & (lane < Z0 + depth), moved, bg[pl.ds(y, xl, stride=yl), :])
        co[y] = DT / perm
    turn[0:yl, 0:xl] = sp[...]
    prof_t[...] = jnp.transpose(turn[...])[0:xl]
    low_x = gx == 0
    x8 = pl.multiple_of(jnp.where(low_x, xl - 8, 0), 8)

    def beside(name, c, y, x, count):
        if name == "co":
            return co[y, pl.ds(x, count), :]
        return refs[name][pl.ds(c * plane + x * yl + y, count, stride=yl), :]

    def beyond(up):
        def rows(name, c, i, x, count):
            if name == "co":
                return co[jnp.where(up, yl - 1 - i, i), pl.ds(x, count), :]
            e, h, h1 = (fe, fh, fh1) if name in FWD else (ae, ah, ah1)
            return edge_row(e, h, h1, name in ("fh", "ah"), c, i, up, x, count, xl, yl)
        return rows

    def windows(parts, x, count, rows):
        out = []
        here = lax.broadcasted_iota(jnp.int32, (count, 128), 1)
        for t in range(ceil(len(parts), PER)):
            acc = jnp.zeros((count, 128), F32)
            for q, (name, c, i) in enumerate(parts[t * PER : (t + 1) * PER]):
                moved = pltpu.roll(rows(name, c, i, x, count), (WIN * q + first) % 128, 1)
                acc = jnp.where((here >= WIN * q) & (here < WIN * (q + 1)), moved, acc)
            out.append(acc)
        return out

    def tiles(dst, raw, win, rows):
        for n, (name, c, i) in enumerate(raw):
            half = pltpu.roll(rows(name, c, i, x8, 8), jnp.where(low_x, 4, 0), 0)[0:4]
            dst[n // 2, 4 * (n % 2) : 4 * (n % 2) + 4, :] = half
        at = ceil(len(raw), 2)
        for tile in windows(win, x8, 8, rows):
            dst[at] = tile
            at += 1
        return at

    for dst, corner, up in ((fa, da, gy % 2 == 0), (fb, db, gy % 2 == 1)):
        rows = beyond(up)
        for u, (name, c, i) in enumerate(F_RAW):
            dst[u] = rows(name, c, i, 0, xl)
        at = len(F_RAW)
        for unit in windows(F_WIN, 0, xl, rows):
            dst[at] = unit
            at += 1
        mix = dst[at - 1]
        prof = prof_t[...]
        for i in range(FH):
            col = jnp.where(up, prof[:, yl - 1 - i : yl - i], prof[:, i : i + 1])
            mix = jnp.where(lane == PROF + i, jnp.broadcast_to(col, (xl, 128)), mix)
        dst[at - 1] = mix
        last = tiles(corner, C_RAW, C_WIN, rows)
        src8 = dst[at - 1, pl.ds(x8, 8), :]
        corner[last - 1] = jnp.where((lane8 >= PROF) & (lane8 < PROF + FH), src8, corner[last - 1])
    raw, win = x_parts(yl)
    last = tiles(px, raw, win, beside)
    px[last] = prof_t[pl.ds(x8, 8), :]


class Halo:
    def __init__(self, mon, xl, yl, put):
        self.xl, self.yl, self.put = xl, yl, put
        self.gx, self.gy = lax.axis_index("gx"), lax.axis_index("gy")
        self.back = mon - WIN // 2 + 256
        sub = lax.broadcasted_iota(jnp.int32, (8, 128), 0)
        low = self.gx == 0
        mask = lambda lo, hi: jnp.where(low, lo.astype(F32), hi.astype(F32))
        self.keep = mask(sub < FH, sub >= 8 - FH)
        self.near = mask(sub < 4, sub >= 4) > 0.5
        self.far = mask((sub >= 4) & (sub < FH), (sub < 4) & (sub >= 8 - FH)) > 0.5
        self.shift = [jnp.where(low, 0, 4), jnp.where(low, 4, 0)]

    def row(self, i, high):
        return jnp.where(high, FH + self.yl + i, FH - 1 - i)

    def unroll(self, tile, q):
        return pltpu.roll(tile, (self.back - WIN * q) % 128, 1)

    def side(self, ref, raw, win, high):
        own = pl.ds(0, self.xl)
        for u, (name, c, i) in enumerate(raw):
            self.put(name, c, self.row(i, high), own, ref[u])
        for s, (name, c, i) in enumerate(win):
            self.put(name, c, self.row(i, high), own, self.unroll(ref[len(raw) + s // PER], s % PER))

    def tiles(self, ref, raw, win, names, where):
        halo = pl.ds(self.xl, 8)
        seats = {part: s for s, part in enumerate(win)}
        at = ceil(len(raw), 2)
        for n, part in enumerate(raw):
            if part[0] not in names:
                continue
            value = jnp.where(self.near, pltpu.roll(ref[n // 2], self.shift[n % 2], 0), 0.0)
            if part in seats:
                s = seats.pop(part)
                value = jnp.where(self.far, self.unroll(ref[at + s // PER], s % PER), value)
            self.put(part[0], part[1], where(part[2]), halo, value)
        for part, s in seats.items():
            if part[0] in names:
                self.put(part[0], part[1], where(part[2]), halo, self.unroll(ref[at + s // PER], s % PER) * self.keep)


class Stepper:
    def __init__(self, xl, yl, cx):
        self.xr = xr = xl + 8
        self.cx = cx
        gx, gy = lax.axis_index("gx"), lax.axis_index("gy")
        self.lane = lax.broadcasted_iota(jnp.int32, (xr, 128), 1)
        ring = lax.broadcasted_iota(jnp.int32, (xr, 128), 0)
        inside_low = jnp.where(ring < xl + FH, F32(DT), F32(0.0))
        inside_high = jnp.where((ring < xl) | (ring >= xr - FH), F32(DT), F32(0.0))
        self.h_in = jnp.where(gx == 0, inside_low, inside_high)
        self.h_low = self.h_in * jnp.where(gy == 0, 0.0, 1.0).astype(F32)
        edge = ((ring == xl - 1) | (ring == xr - 1)).astype(F32)
        self.h_edge = self.h_in * edge
        self.z_last = self.lane == 127
        ri = lax.broadcasted_iota(jnp.int32, (128, 128), 0)
        ci = lax.broadcasted_iota(jnp.int32, (128, 128), 1)
        diff = jnp.where(ri == ci, F32(1.0), F32(0.0)) - jnp.where(ri == ci - 1, F32(1.0), F32(0.0))
        self.diff = jnp.concatenate([diff] * 3, 0).astype(BF16)

    def zdn(self, p, q):
        v = jnp.concatenate([p, q], 0)
        hi = v.astype(BF16)
        rest = v - hi.astype(F32)
        mid = rest.astype(BF16)
        low = (rest - mid.astype(F32)).astype(BF16)
        out = lax.dot_general(jnp.concatenate([hi, mid, low], 1), self.diff, (((1,), (0,)), ((), ())),
                              preferred_element_type=F32)
        return out[0 : self.xr], out[self.xr :]

    def zup(self, v):
        return jnp.where(self.z_last, 0.0, pltpu.roll(v, 127, 1)) - v

    def xup(self, v):
        return pltpu.roll(v, self.xr - 1, 0) - v

    def xdn(self, v):
        return v - pltpu.roll(v, 1, 0)

    def rows(self, e, h, start, stop, given=()):
        load = lambda ref, y: (ref[0, y], ref[1, y], ref[2, y])
        cur, now = load(e, start), None
        for y in range(start, stop):
            up = load(e, y + 1)
            below = now
            k = self.h_low if y < FH else self.h_in
            ex, ey, ez = cur
            if y in given:
                k = self.h_edge
                now = (
                    h[0, y],
                    h[1, y] + k * pltpu.roll(ez, self.xr - 1, 0),
                    h[2, y] - k * pltpu.roll(ey, self.xr - 1, 0),
                )
            else:
                now = (
                    h[0, y] - k * ((up[2] - ez) - self.zup(ey)),
                    h[1, y] - k * (self.zup(ex) - self.xup(ez)),
                    h[2, y] - k * (self.xup(ey) - (up[0] - ex)),
                )
            for c in range(3):
                h[c, y] = now[c]
            if y > start:
                hx, hy, hz = now
                k = self.cx[y]
                zy, zx = self.zdn(hy, hx)
                yield y, cur, (
                    k * ((hz - below[2]) - zy),
                    k * (zx - self.xdn(hz)),
                    k * (self.xdn(hy) - (hx - below[0])),
                )
            cur = up


def given_rows(yl):
    return {FH - 3, FH - 2, *range(FH + yl, yl + 2 * FH)}


def pick(values):
    w = lax.axis_index("wl")
    value = F32(values[0])
    for i in range(1, len(values)):
        value = jnp.where(w == i, F32(values[i]), value)
    return value


def fill_own(refs, bigs, xl, yl):
    for ref, big in zip(refs, bigs):
        for c in range(3):
            for y in range(yl):
                big[c, FH + y, 0:xl, :] = ref[pl.ds(c * xl * yl + y, xl, stride=yl), :]


def put_out(big, out, xl, yl):
    for c in range(3):
        for y in range(yl):
            out[pl.ds(c * xl * yl + y, xl, stride=yl), :] = big[c, FH + y, 0:xl, :]


def store_body(e3, a, out_f, out_a, *, xl, yl):
    put_out(e3, out_f, xl, yl)
    put_out(a, out_a, xl, yl)


def forward_body(src, mon, fe, fh, co, prof_t, ra, rb, rx, rda, rdb, cx, e1, e2, e3, e0, h, sx, *, xl, yl, signals):
    xr, yr = xl + 8, yl + 2 * FH
    gy = lax.axis_index("gy")
    src_l = src[0]
    own, halo = pl.ds(0, xl), pl.ds(xl, 8)

    def put(name, c, row, cols, value):
        if name == "co":
            cx[row, cols, :] = value
        else:
            (e0 if name == "fe" else h)[c, row, cols, :] = value

    to = Halo(mon[0], xl, yl, put)
    fill_own((fe, fh), (e0, h), xl, yl)
    for y in range(yl):
        cx[FH + y, own, :] = co[y]
    names = FWD + ("co",)
    raw, win = x_parts(yl)
    to.tiles(rx, raw, win, names, lambda y: FH + y)
    at_src = lax.broadcasted_iota(jnp.int32, (xl, 128), 1) == src_l
    at_src8 = lax.broadcasted_iota(jnp.int32, (8, 128), 1) == src_l

    def source(row, wide, tile, lane):
        sx[row, own, :] = jnp.where(at_src, jnp.broadcast_to(wide[:, lane : lane + 1], (xl, 128)), 0.0)
        sx[row, halo, :] = jnp.where(at_src8, jnp.broadcast_to(tile[:, lane : lane + 1], (8, 128)), 0.0)

    prof, prof_x = prof_t[...], rx[rx.shape[0] - 1] * to.keep
    for y in range(yl):
        source(FH + y, prof, prof_x, y)
    for ref, ref_d, high in ((ra, rda, gy % 2 == 0), (rb, rdb, gy % 2 == 1)):
        to.side(ref, F_RAW, F_WIN, high)
        to.tiles(ref_d, C_RAW, C_WIN, names, lambda i, high=high: to.row(i, high))
        prof_y, prof_d = ref[ref.shape[0] - 1], ref_d[ref_d.shape[0] - 1] * to.keep
        for i in range(FH):
            source(to.row(i, high), prof_y, prof_d, PROF + i)
    step = Stepper(xl, yl, cx)
    runs = (e0, e1, e2, e3)
    for k in range(STEPS):
        new = runs[k + 1]
        signal = pick([s[k] for s in signals])
        for y, cur, inc in step.rows(runs[k], h, k, yr - 1 - k, given_rows(yl) if k == 0 else ()):
            new[0, y] = cur[0] + inc[0] + signal * sx[y]
            new[1, y] = cur[1] + inc[1]
            new[2, y] = cur[2] + inc[2]


def adjoint_body(mon, ae, ah, cx, e1, e2, e3, ra, rb, rx, rda, rdb, a, grad, g, *, xl, yl, omegas):
    yr = yl + 2 * FH
    gy = lax.axis_index("gy")

    def put(name, c, row, cols, value):
        (a if name == "ae" else g)[c, row, cols, :] = value

    to = Halo(mon[0], xl, yl, put)
    for c in range(3):
        a[c, FH - AH] = jnp.zeros((xl + 8, 128), F32)
    fill_own((ae, ah), (a, g), xl, yl)
    raw, win = x_parts(yl)
    to.tiles(rx, raw, win, ADJ, lambda y: FH + y)
    for ref, ref_d, high in ((ra, rda, gy % 2 == 0), (rb, rdb, gy % 2 == 1)):
        to.side(ref, A_RAW, [], high)
        to.tiles(ref_d, C_RAW, C_WIN, ADJ, lambda i, high=high: to.row(i, high))
    step = Stepper(xl, yl, cx)
    at_mon = step.lane == mon[0]
    total = [None] * yl
    for j in range(STEPS):
        seen = (e3, e2, e1)[j]
        for y, cur, inc in step.rows(a, g, FH - AH + j, yr - AH - j, given_rows(yl) if j == 0 else ()):
            for c in range(3):
                f = seen[c, y]
                v = cur[c] + inc[c] + jnp.where(at_mon, 2.0 * DT * f, 0.0)
                a[c, y] = v
                if FH <= y < FH + yl:
                    t = (f * v)[0:xl]
                    i = y - FH
                    total[i] = t if total[i] is None else total[i] + t
    scale = pick([o * o for o in omegas])
    lane = step.lane[0:xl]
    packed = jnp.zeros((xl, 128), F32)
    wide = 128 // yl
    for y in range(yl):
        moved = pltpu.roll(total[y] * scale, (wide * y - Z0) % 128, 1)
        packed = jnp.where((lane >= wide * y) & (lane < wide * (y + 1)), moved, packed)
    grad[...] = packed


def sum_body(*refs, owned, xl, yl):
    *parts, out, turn = refs
    w = lax.axis_index("wl")
    acc = parts[0][...]
    for p in parts[1:]:
        acc = acc + p[...]
    turn[...] = jnp.transpose(acc)
    for i in range(owned):
        out[i] = turn[pl.ds(owned * w + i, yl, stride=128 // yl), :]


def per_device(fe, fh, ae, ah, background, design, source_profile, source_layer, monitor_layer):
    _, _, xl, yl, nz = fe.shape
    nw = lax.axis_size("wl")
    owned = design.shape[0]
    xr, yr = xl + 8, yl + 2 * FH
    flat = [v.reshape(3 * xl * yl, nz) for v in (fe, fh, ae, ah)] + [background.reshape(xl * yl, nz)]
    sp = jnp.transpose(source_profile[0])
    shape = lambda *s: jax.ShapeDtypeStruct(s, F32)
    smem = pl.BlockSpec(memory_space=pltpu.SMEM)
    vmem = pl.BlockSpec(memory_space=pltpu.VMEM)
    hbm = pl.BlockSpec(memory_space=pltpu.HBM)
    ext = lambda *s: pltpu.VMEM(s, F32)
    field = (3, yr, xr, nz)

    def call(body, name, out, specs, scratch=()):
        return pl.pallas_call(
            body, out_shape=tuple(shape(*s) for s in out), in_specs=specs, out_specs=(vmem,) * len(out),
            scratch_shapes=list(scratch), name=name,
            compiler_params=pltpu.CompilerParams(vmem_limit_bytes=20 * 1024 * 1024),
        )

    def over_wl(v):
        return [v] + [lax.ppermute(v, "wl", [(i, i ^ k) for i in range(nw)]) for k in range(1, nw)]

    raw, win = x_parts(yl)
    f_side = (len(F_RAW) + ceil(len(F_WIN), PER), xl, nz)
    a_side = (len(A_RAW), xl, nz)
    corner = (ceil(len(C_RAW), 2) + ceil(len(C_WIN), PER), 8, nz)
    beside = (ceil(len(raw), 2) + ceil(len(win), PER) + 1, 8, nz)

    layers = over_wl(jnp.transpose(design, (0, 2, 1)))
    fe, fh, ae, ah, bg = flat
    h1 = (3, yl, xl, nz)
    ae, ah, fe, fh, bg, ah1, aa, ab = call(
        lambda *r: fetch_body(*r, xl=xl, yl=yl), "fetch",
        [ae.shape] * 4 + [bg.shape, h1, a_side, a_side], [hbm] * 5, [pltpu.SemaphoreType.DMA((5,))],
    )(*[pltpu.with_memory_space_constraint(v, pltpu.HBM) for v in (ae, ah, fe, fh, bg)])
    raa, rab = swap(aa, False, 0), swap(ab, False, 1)
    (fh1,) = call(lambda *r: first_body(*r, xl=xl, yl=yl), "first", [h1], [vmem] * 2)(fe, fh)
    co, prof_t, fa, fb, px, da, db = call(
        lambda *r: send_body(*r, xl=xl, yl=yl, nw=nw, owned=owned), "send",
        [(yl, xl, nz), (xl, nz), f_side, f_side, beside, corner, corner],
        [smem] + [vmem] * (8 + nw), [ext(128, 128)],
    )(monitor_layer, fe, fh, ae, ah, bg, fh1, ah1, sp, *layers)
    rfa, rfb = swap(fa, False, 0), swap(fb, False, 1)
    rx = swap(px, True, None)
    rda, rdb = swap(da, True, 0), swap(db, True, 1)
    f32 = np.float32
    omegas = [f32(2.0 * math.pi) / (f32(16.0) + f32(32.0) * f32(i) / f32(nw)) for i in range(nw)]
    signals = [[f32(DT) * np.sin(f32(o * f32((k + 1) * DT))) for k in range(STEPS)] for o in omegas]
    cx, e1, e2, e3 = call(
        lambda *r: forward_body(*r, xl=xl, yl=yl, signals=signals), "forward",
        [(yr, xr, nz), field, field, field], [smem, smem] + [vmem] * 9,
        [ext(*field), ext(*field), ext(yr, xr, nz)],
    )(source_layer, monitor_layer, fe, fh, co, prof_t, rfa, rfb, rx, rda, rdb)
    last_a, grad = call(
        lambda *r: adjoint_body(*r, xl=xl, yl=yl, omegas=omegas), "adjoint",
        [field, (xl, nz)], [smem] + [vmem] * 11, [ext(*field)],
    )(monitor_layer, ae, ah, cx, e1, e2, e3, raa, rab, rx, rda, rdb)
    terms = over_wl(grad)
    out_f, out_a = call(
        lambda *r: store_body(*r, xl=xl, yl=yl), "store", [flat[0].shape] * 2, [vmem] * 2)(e3, last_a)
    (gradient,) = call(
        lambda *r: sum_body(*r, owned=owned, xl=xl, yl=yl), "gather_sum",
        [(owned, yl, xl)], [vmem] * nw, [ext(128, xl)],
    )(*terms)
    block = (1, 3, xl, yl, nz)
    return (out_f.reshape(block), out_a.reshape(block), jnp.transpose(gradient, (0, 2, 1)))


def solution(mesh):
    field = P("wl", None, "gx", "gy", None)
    return jax.shard_map(
        per_device,
        mesh=mesh,
        in_specs=(field, field, field, field, P("gx", "gy", None), P("wl", "gx", "gy"),
                  P("wl", "gx", "gy"), P("wl"), P("wl")),
        out_specs=(field, field, P("wl", "gx", "gy")),
        check_vma=False,
    )
```

```python
import math

import jax
import jax.numpy as jnp
import numpy as np
from jax import lax
from jax.experimental import pallas as pl
from jax.experimental.pallas import tpu as pltpu
from jax.sharding import PartitionSpec as P

Z0 = 64
STEPS = 3
DT = 0.5
F32 = jnp.float32
BF16 = jnp.bfloat16
FH = 5
AH = 3
WIN = 8
PER = 128 // WIN
PROF = 112


def swap(block, flip_x, parity):
    nx, ny = lax.axis_size("gx"), lax.axis_size("gy")
    route = []
    for a in range(nx):
        for b in range(ny):
            ta = a ^ 1 if flip_x else a
            tb = b if parity is None else ((b + parity) ^ 1) - parity
            if 0 <= ta < nx and 0 <= tb < ny:
                route.append((a * ny + b, ta * ny + tb))
    return lax.ppermute(block, ("gx", "gy"), route)


FWD, ADJ = ("fe", "fh"), ("ae", "ah")
def side_parts(e, h):
    return [(e, c, i) for c in range(3) for i in range(2)] + [(h, c, i) for c in range(3) for i in range(2)] + [(h, 0, 2), (h, 2, 2)]


CO_RAW, CO_WIN = [("co", 0, i) for i in (0, 1)], [("co", 0, i) for i in (2, 3)]
F_RAW = side_parts(*FWD) + CO_RAW
A_RAW = side_parts(*ADJ)
F_WIN = [("fe", c, i) for c in range(3) for i in (2, 3, 4)] + [("fh", 1, 2)]
F_WIN += [("fh", c, i) for c in range(3) for i in (3, 4)] + CO_WIN
C_RAW = side_parts(*FWD) + [("fe", 1, 2)] + A_RAW + [("ae", 1, 2)] + CO_RAW
C_WIN = [(n, c, i) for n in FWD for c in range(3) for i in range(FH)] + CO_RAW + CO_WIN


def x_parts(yl):
    raw = [(n, c, y) for n in FWD + ADJ for c in range(3) for y in range(yl)]
    win = [(n, c, y) for n in FWD for c in range(3) for y in range(yl)]
    co = [("co", 0, y) for y in range(yl)]
    return raw + co, win + co


def ceil(a, b):
    return -(-a // b)


def stepped(e, h, out, xl, yl):
    sub = lax.broadcasted_iota(jnp.int32, (xl, 128), 0)
    x_last = sub == xl - 1
    z_last = lax.broadcasted_iota(jnp.int32, (xl, 128), 1) == 127
    zup = lambda v: jnp.where(z_last, 0.0, pltpu.roll(v, 127, 1)) - v
    xup = lambda v: jnp.where(x_last, 0.0, pltpu.roll(v, xl - 1, 0)) - v
    row = lambda ref, c, y: ref[pl.ds(c * xl * yl + y, xl, stride=yl), :]
    cur = [row(e, c, 0) for c in range(3)]
    for y in range(yl - 1):
        up = [row(e, c, y + 1) for c in range(3)]
        ex, ey, ez = cur
        out[0, y] = row(h, 0, y) - DT * ((up[2] - ez) - zup(ey))
        out[1, y] = row(h, 1, y) - DT * (zup(ex) - xup(ez))
        out[2, y] = row(h, 2, y) - DT * (xup(ey) - (up[0] - ex))
        cur = up


def edge_row(e, h, h1, is_h, c, i, up, x, count, xl, yl):
    here = jnp.where(up, yl - 1 - i, i)
    flat = lambda ref, r: ref[pl.ds(c * xl * yl + x * yl + r, count, stride=yl), :]
    if not is_h:
        return flat(e, here)
    if i in (1, 2):
        return h1[c, here, pl.ds(x, count), :]
    return jnp.where(up, flat(h, yl - 1 - i), h1[c, i, pl.ds(x, count), :])


def fetch_body(ae, ah, fe, fh, bg, *rest, xl, yl):
    outs, (h1, aa, ab, sems) = rest[:5], rest[5:]
    copies = [pltpu.make_async_copy(s, d, sems.at[i]) for i, (s, d) in enumerate(zip((ae, ah, fe, fh, bg), outs))]
    for c in copies:
        c.start()
    copies[0].wait()
    copies[1].wait()
    e, h = outs[0], outs[1]
    gy = lax.axis_index("gy")
    stepped(e, h, h1, xl, yl)
    for u, (name, c, i) in enumerate(A_RAW):
        for dst, up in ((aa, gy % 2 == 0), (ab, gy % 2 == 1)):
            dst[u] = edge_row(e, h, h1, name == "ah", c, i, up, 0, xl, xl, yl)
    for c in copies[2:]:
        c.wait()


def first_body(fe, fh, h1, *, xl, yl):
    stepped(fe, fh, h1, xl, yl)


def send_body(mon, fe, fh, ae, ah, bg, fh1, ah1, sp, *rest, xl, yl, nw, owned):
    parts, (co, prof_t, fa, fb, px, da, db, turn) = rest[:nw], rest[nw:]
    gx, gy, w = lax.axis_index("gx"), lax.axis_index("gy"), lax.axis_index("wl")
    plane = xl * yl
    depth = nw * owned
    lane = lax.broadcasted_iota(jnp.int32, (xl, 128), 1)
    lane8 = lane[0:8]
    first = WIN // 2 - mon[0] + 256
    refs = dict(fe=fe, fh=fh, ae=ae, ah=ah)
    turn[...] = jnp.zeros((128, 128), F32)
    for k in range(nw):
        for i in range(owned):
            turn[pl.ds(owned * (w ^ k) + i, yl, stride=depth), 0:xl] = parts[k][i]
    layers = jnp.transpose(turn[...])[0:xl]
    for y in range(yl):
        moved = pltpu.roll(layers, (Z0 - depth * y) % 128, 1)
        perm = jnp.where((lane >= Z0) & (lane < Z0 + depth), moved, bg[pl.ds(y, xl, stride=yl), :])
        co[y] = DT / perm
    turn[0:yl, 0:xl] = sp[...]
    prof_t[...] = jnp.transpose(turn[...])[0:xl]
    low_x = gx == 0
    x8 = pl.multiple_of(jnp.where(low_x, xl - 8, 0), 8)

    def beside(name, c, y, x, count):
        if name == "co":
            return co[y, pl.ds(x, count), :]
        return refs[name][pl.ds(c * plane + x * yl + y, count, stride=yl), :]

    def beyond(up):
        def rows(name, c, i, x, count):
            if name == "co":
                return co[jnp.where(up, yl - 1 - i, i), pl.ds(x, count), :]
            e, h, h1 = (fe, fh, fh1) if name in FWD else (ae, ah, ah1)
            return edge_row(e, h, h1, name in ("fh", "ah"), c, i, up, x, count, xl, yl)
        return rows

    def windows(parts, x, count, rows):
        out = []
        here = lax.broadcasted_iota(jnp.int32, (count, 128), 1)
        for t in range(ceil(len(parts), PER)):
            acc = jnp.zeros((count, 128), F32)
            for q, (name, c, i) in enumerate(parts[t * PER : (t + 1) * PER]):
                moved = pltpu.roll(rows(name, c, i, x, count), (WIN * q + first) % 128, 1)
                acc = jnp.where((here >= WIN * q) & (here < WIN * (q + 1)), moved, acc)
            out.append(acc)
        return out

    def tiles(dst, raw, win, rows):
        for n, (name, c, i) in enumerate(raw):
            half = pltpu.roll(rows(name, c, i, x8, 8), jnp.where(low_x, 4, 0), 0)[0:4]
            dst[n // 2, 4 * (n % 2) : 4 * (n % 2) + 4, :] = half
        at = ceil(len(raw), 2)
        for tile in windows(win, x8, 8, rows):
            dst[at] = tile
            at += 1
        return at

    for dst, corner, up in ((fa, da, gy % 2 == 0), (fb, db, gy % 2 == 1)):
        rows = beyond(up)
        for u, (name, c, i) in enumerate(F_RAW):
            dst[u] = rows(name, c, i, 0, xl)
        at = len(F_RAW)
        for unit in windows(F_WIN, 0, xl, rows):
            dst[at] = unit
            at += 1
        mix = dst[at - 1]
        prof = prof_t[...]
        for i in range(FH):
            col = jnp.where(up, prof[:, yl - 1 - i : yl - i], prof[:, i : i + 1])
            mix = jnp.where(lane == PROF + i, jnp.broadcast_to(col, (xl, 128)), mix)
        dst[at - 1] = mix
        last = tiles(corner, C_RAW, C_WIN, rows)
        src8 = dst[at - 1, pl.ds(x8, 8), :]
        corner[last - 1] = jnp.where((lane8 >= PROF) & (lane8 < PROF + FH), src8, corner[last - 1])
    raw, win = x_parts(yl)
    last = tiles(px, raw, win, beside)
    px[last] = prof_t[pl.ds(x8, 8), :]


class Halo:
    def __init__(self, mon, xl, yl, put):
        self.xl, self.yl, self.put = xl, yl, put
        self.gx, self.gy = lax.axis_index("gx"), lax.axis_index("gy")
        self.back = mon - WIN // 2 + 256
        sub = lax.broadcasted_iota(jnp.int32, (8, 128), 0)
        low = self.gx == 0
        mask = lambda lo, hi: jnp.where(low, lo.astype(F32), hi.astype(F32))
        self.keep = mask(sub < FH, sub >= 8 - FH)
        self.near = mask(sub < 4, sub >= 4) > 0.5
        self.far = mask((sub >= 4) & (sub < FH), (sub < 4) & (sub >= 8 - FH)) > 0.5
        self.shift = [jnp.where(low, 0, 4), jnp.where(low, 4, 0)]

    def row(self, i, high):
        return jnp.where(high, FH + self.yl + i, FH - 1 - i)

    def unroll(self, tile, q):
        return pltpu.roll(tile, (self.back - WIN * q) % 128, 1)

    def side(self, ref, raw, win, high):
        own = pl.ds(0, self.xl)
        for u, (name, c, i) in enumerate(raw):
            self.put(name, c, self.row(i, high), own, ref[u])
        for s, (name, c, i) in enumerate(win):
            self.put(name, c, self.row(i, high), own, self.unroll(ref[len(raw) + s // PER], s % PER))

    def tiles(self, ref, raw, win, names, where):
        halo = pl.ds(self.xl, 8)
        seats = {part: s for s, part in enumerate(win)}
        at = ceil(len(raw), 2)
        for n, part in enumerate(raw):
            if part[0] not in names:
                continue
            value = jnp.where(self.near, pltpu.roll(ref[n // 2], self.shift[n % 2], 0), 0.0)
            if part in seats:
                s = seats.pop(part)
                value = jnp.where(self.far, self.unroll(ref[at + s // PER], s % PER), value)
            self.put(part[0], part[1], where(part[2]), halo, value)
        for part, s in seats.items():
            if part[0] in names:
                self.put(part[0], part[1], where(part[2]), halo, self.unroll(ref[at + s // PER], s % PER) * self.keep)


class Stepper:
    def __init__(self, xl, yl, cx):
        self.xr = xr = xl + 8
        self.cx = cx
        gx, gy = lax.axis_index("gx"), lax.axis_index("gy")
        self.lane = lax.broadcasted_iota(jnp.int32, (xr, 128), 1)
        ring = lax.broadcasted_iota(jnp.int32, (xr, 128), 0)
        inside_low = jnp.where(ring < xl + FH, F32(DT), F32(0.0))
        inside_high = jnp.where((ring < xl) | (ring >= xr - FH), F32(DT), F32(0.0))
        self.h_in = jnp.where(gx == 0, inside_low, inside_high)
        self.h_low = self.h_in * jnp.where(gy == 0, 0.0, 1.0).astype(F32)
        edge = ((ring == xl - 1) | (ring == xr - 1)).astype(F32)
        self.h_edge = self.h_in * edge
        self.z_last = self.lane == 127
        ri = lax.broadcasted_iota(jnp.int32, (128, 128), 0)
        ci = lax.broadcasted_iota(jnp.int32, (128, 128), 1)
        diff = jnp.where(ri == ci, F32(1.0), F32(0.0)) - jnp.where(ri == ci - 1, F32(1.0), F32(0.0))
        self.diff = jnp.concatenate([diff] * 3, 0).astype(BF16)

    def zdn(self, p, q):
        v = jnp.concatenate([p, q], 0)
        hi = v.astype(BF16)
        rest = v - hi.astype(F32)
        mid = rest.astype(BF16)
        low = (rest - mid.astype(F32)).astype(BF16)
        out = lax.dot_general(jnp.concatenate([hi, mid, low], 1), self.diff, (((1,), (0,)), ((), ())),
                              preferred_element_type=F32)
        return out[0 : self.xr], out[self.xr :]

    def zup(self, v):
        return jnp.where(self.z_last, 0.0, pltpu.roll(v, 127, 1)) - v

    def xup(self, v):
        return pltpu.roll(v, self.xr - 1, 0) - v

    def xdn(self, v):
        return v - pltpu.roll(v, 1, 0)

    def rows(self, e, h, start, stop, given=()):
        load = lambda ref, y: (ref[0, y], ref[1, y], ref[2, y])
        cur, now = load(e, start), None
        for y in range(start, stop):
            up = load(e, y + 1)
            below = now
            k = self.h_low if y < FH else self.h_in
            ex, ey, ez = cur
            if y in given:
                k = self.h_edge
                now = (
                    h[0, y],
                    h[1, y] + k * pltpu.roll(ez, self.xr - 1, 0),
                    h[2, y] - k * pltpu.roll(ey, self.xr - 1, 0),
                )
            else:
                now = (
                    h[0, y] - k * ((up[2] - ez) - self.zup(ey)),
                    h[1, y] - k * (self.zup(ex) - self.xup(ez)),
                    h[2, y] - k * (self.xup(ey) - (up[0] - ex)),
                )
            for c in range(3):
                h[c, y] = now[c]
            if y > start:
                hx, hy, hz = now
                k = self.cx[y]
                zy, zx = self.zdn(hy, hx)
                yield y, cur, (
                    k * ((hz - below[2]) - zy),
                    k * (zx - self.xdn(hz)),
                    k * (self.xdn(hy) - (hx - below[0])),
                )
            cur = up


def given_rows(yl):
    return {FH - 3, FH - 2, *range(FH + yl, yl + 2 * FH)}


def pick(values):
    w = lax.axis_index("wl")
    value = F32(values[0])
    for i in range(1, len(values)):
        value = jnp.where(w == i, F32(values[i]), value)
    return value


def fill_own(refs, bigs, xl, yl):
    for ref, big in zip(refs, bigs):
        for c in range(3):
            for y in range(yl):
                big[c, FH + y, 0:xl, :] = ref[pl.ds(c * xl * yl + y, xl, stride=yl), :]


def put_out(big, out, xl, yl):
    for c in range(3):
        for y in range(yl):
            out[pl.ds(c * xl * yl + y, xl, stride=yl), :] = big[c, FH + y, 0:xl, :]


def store_body(e3, a, out_f, out_a, *, xl, yl):
    put_out(e3, out_f, xl, yl)
    put_out(a, out_a, xl, yl)


def forward_body(src, mon, fe, fh, co, prof_t, ra, rb, rx, rda, rdb, cx, e1, e2, e3, e0, h, sx, *, xl, yl, signals):
    xr, yr = xl + 8, yl + 2 * FH
    gy = lax.axis_index("gy")
    src_l = src[0]
    own, halo = pl.ds(0, xl), pl.ds(xl, 8)

    def put(name, c, row, cols, value):
        if name == "co":
            cx[row, cols, :] = value
        else:
            (e0 if name == "fe" else h)[c, row, cols, :] = value

    to = Halo(mon[0], xl, yl, put)
    fill_own((fe, fh), (e0, h), xl, yl)
    for y in range(yl):
        cx[FH + y, own, :] = co[y]
    names = FWD + ("co",)
    raw, win = x_parts(yl)
    to.tiles(rx, raw, win, names, lambda y: FH + y)
    at_src = lax.broadcasted_iota(jnp.int32, (xl, 128), 1) == src_l
    at_src8 = lax.broadcasted_iota(jnp.int32, (8, 128), 1) == src_l

    def source(row, wide, tile, lane):
        sx[row, own, :] = jnp.where(at_src, jnp.broadcast_to(wide[:, lane : lane + 1], (xl, 128)), 0.0)
        sx[row, halo, :] = jnp.where(at_src8, jnp.broadcast_to(tile[:, lane : lane + 1], (8, 128)), 0.0)

    prof, prof_x = prof_t[...], rx[rx.shape[0] - 1] * to.keep
    for y in range(yl):
        source(FH + y, prof, prof_x, y)
    for ref, ref_d, high in ((ra, rda, gy % 2 == 0), (rb, rdb, gy % 2 == 1)):
        to.side(ref, F_RAW, F_WIN, high)
        to.tiles(ref_d, C_RAW, C_WIN, names, lambda i, high=high: to.row(i, high))
        prof_y, prof_d = ref[ref.shape[0] - 1], ref_d[ref_d.shape[0] - 1] * to.keep
        for i in range(FH):
            source(to.row(i, high), prof_y, prof_d, PROF + i)
    step = Stepper(xl, yl, cx)
    runs = (e0, e1, e2, e3)
    for k in range(STEPS):
        new = runs[k + 1]
        signal = pick([s[k] for s in signals])
        for y, cur, inc in step.rows(runs[k], h, k, yr - 1 - k, given_rows(yl) if k == 0 else ()):
            new[0, y] = cur[0] + inc[0] + signal * sx[y]
            new[1, y] = cur[1] + inc[1]
            new[2, y] = cur[2] + inc[2]


def adjoint_body(mon, ae, ah, cx, e1, e2, e3, ra, rb, rx, rda, rdb, a, grad, g, *, xl, yl, omegas):
    yr = yl + 2 * FH
    gy = lax.axis_index("gy")

    def put(name, c, row, cols, value):
        (a if name == "ae" else g)[c, row, cols, :] = value

    to = Halo(mon[0], xl, yl, put)
    for c in range(3):
        a[c, FH - AH] = jnp.zeros((xl + 8, 128), F32)
    fill_own((ae, ah), (a, g), xl, yl)
    raw, win = x_parts(yl)
    to.tiles(rx, raw, win, ADJ, lambda y: FH + y)
    for ref, ref_d, high in ((ra, rda, gy % 2 == 0), (rb, rdb, gy % 2 == 1)):
        to.side(ref, A_RAW, [], high)
        to.tiles(ref_d, C_RAW, C_WIN, ADJ, lambda i, high=high: to.row(i, high))
    step = Stepper(xl, yl, cx)
    at_mon = step.lane == mon[0]
    total = [None] * yl
    for j in range(STEPS):
        seen = (e3, e2, e1)[j]
        for y, cur, inc in step.rows(a, g, FH - AH + j, yr - AH - j, given_rows(yl) if j == 0 else ()):
            for c in range(3):
                f = seen[c, y]
                v = cur[c] + inc[c] + jnp.where(at_mon, 2.0 * DT * f, 0.0)
                a[c, y] = v
                if FH <= y < FH + yl:
                    t = (f * v)[0:xl]
                    i = y - FH
                    total[i] = t if total[i] is None else total[i] + t
    scale = pick([o * o for o in omegas])
    lane = step.lane[0:xl]
    packed = jnp.zeros((xl, 128), F32)
    wide = 128 // yl
    for y in range(yl):
        moved = pltpu.roll(total[y] * scale, (wide * y - Z0) % 128, 1)
        packed = jnp.where((lane >= wide * y) & (lane < wide * (y + 1)), moved, packed)
    grad[...] = packed


def sum_body(*refs, owned, xl, yl):
    *parts, out, turn = refs
    w = lax.axis_index("wl")
    acc = parts[0][...]
    for p in parts[1:]:
        acc = acc + p[...]
    turn[...] = jnp.transpose(acc)
    for i in range(owned):
        out[i] = turn[pl.ds(owned * w + i, yl, stride=128 // yl), :]


def per_device(fe, fh, ae, ah, background, design, source_profile, source_layer, monitor_layer):
    _, _, xl, yl, nz = fe.shape
    nw = lax.axis_size("wl")
    owned = design.shape[0]
    xr, yr = xl + 8, yl + 2 * FH
    flat = [v.reshape(3 * xl * yl, nz) for v in (fe, fh, ae, ah)] + [background.reshape(xl * yl, nz)]
    sp = jnp.transpose(source_profile[0])
    shape = lambda *s: jax.ShapeDtypeStruct(s, F32)
    smem = pl.BlockSpec(memory_space=pltpu.SMEM)
    vmem = pl.BlockSpec(memory_space=pltpu.VMEM)
    hbm = pl.BlockSpec(memory_space=pltpu.HBM)
    ext = lambda *s: pltpu.VMEM(s, F32)
    field = (3, yr, xr, nz)

    def call(body, name, out, specs, scratch=()):
        return pl.pallas_call(
            body, out_shape=tuple(shape(*s) for s in out), in_specs=specs, out_specs=(vmem,) * len(out),
            scratch_shapes=list(scratch), name=name,
            compiler_params=pltpu.CompilerParams(vmem_limit_bytes=20 * 1024 * 1024),
        )

    def over_wl(v):
        return [v] + [lax.ppermute(v, "wl", [(i, i ^ k) for i in range(nw)]) for k in range(1, nw)]

    raw, win = x_parts(yl)
    f_side = (len(F_RAW) + ceil(len(F_WIN), PER), xl, nz)
    a_side = (len(A_RAW), xl, nz)
    corner = (ceil(len(C_RAW), 2) + ceil(len(C_WIN), PER), 8, nz)
    beside = (ceil(len(raw), 2) + ceil(len(win), PER) + 1, 8, nz)

    layers = over_wl(jnp.transpose(design, (0, 2, 1)))
    fe, fh, ae, ah, bg = flat
    h1 = (3, yl, xl, nz)
    ae, ah, fe, fh, bg, ah1, aa, ab = call(
        lambda *r: fetch_body(*r, xl=xl, yl=yl), "fetch",
        [ae.shape] * 4 + [bg.shape, h1, a_side, a_side], [hbm] * 5, [pltpu.SemaphoreType.DMA((5,))],
    )(*[pltpu.with_memory_space_constraint(v, pltpu.HBM) for v in (ae, ah, fe, fh, bg)])
    raa, rab = swap(aa, False, 0), swap(ab, False, 1)
    (fh1,) = call(lambda *r: first_body(*r, xl=xl, yl=yl), "first", [h1], [vmem] * 2)(fe, fh)
    co, prof_t, fa, fb, px, da, db = call(
        lambda *r: send_body(*r, xl=xl, yl=yl, nw=nw, owned=owned), "send",
        [(yl, xl, nz), (xl, nz), f_side, f_side, beside, corner, corner],
        [smem] + [vmem] * (8 + nw), [ext(128, 128)],
    )(monitor_layer, fe, fh, ae, ah, bg, fh1, ah1, sp, *layers)
    rfa, rfb = swap(fa, False, 0), swap(fb, False, 1)
    rx = swap(px, True, None)
    rda, rdb = swap(da, True, 0), swap(db, True, 1)
    f32 = np.float32
    omegas = [f32(2.0 * math.pi) / (f32(16.0) + f32(32.0) * f32(i) / f32(nw)) for i in range(nw)]
    signals = [[f32(DT) * np.sin(f32(o * f32((k + 1) * DT))) for k in range(STEPS)] for o in omegas]
    cx, e1, e2, e3 = call(
        lambda *r: forward_body(*r, xl=xl, yl=yl, signals=signals), "forward",
        [(yr, xr, nz), field, field, field], [smem, smem] + [vmem] * 9,
        [ext(*field), ext(*field), ext(yr, xr, nz)],
    )(source_layer, monitor_layer, fe, fh, co, prof_t, rfa, rfb, rx, rda, rdb)
    last_a, grad = call(
        lambda *r: adjoint_body(*r, xl=xl, yl=yl, omegas=omegas), "adjoint",
        [field, (xl, nz)], [smem] + [vmem] * 11, [ext(*field)],
    )(monitor_layer, ae, ah, cx, e1, e2, e3, raa, rab, rx, rda, rdb)
    terms = over_wl(grad)
    out_f, out_a = call(
        lambda *r: store_body(*r, xl=xl, yl=yl), "store", [flat[0].shape] * 2, [vmem] * 2)(e3, last_a)
    (gradient,) = call(
        lambda *r: sum_body(*r, owned=owned, xl=xl, yl=yl), "gather_sum",
        [(owned, yl, xl)], [vmem] * nw, [ext(128, xl)],
    )(*terms)
    block = (1, 3, xl, yl, nz)
    return (out_f.reshape(block), out_a.reshape(block), jnp.transpose(gradient, (0, 2, 1)))


def solution(mesh):
    field = P("wl", None, "gx", "gy", None)
    return jax.shard_map(
        per_device,
        mesh=mesh,
        in_specs=(field, field, field, field, P("gx", "gy", None), P("wl", "gx", "gy"),
                  P("wl", "gx", "gy"), P("wl"), P("wl")),
        out_specs=(field, field, P("wl", "gx", "gy")),
        check_vma=False,
    )
```

```python
import math

import jax
import jax.numpy as jnp
import numpy as np
from jax import lax
from jax.experimental import pallas as pl
from jax.experimental.pallas import tpu as pltpu
from jax.sharding import PartitionSpec as P

Z0 = 64
STEPS = 3
DT = 0.5
F32 = jnp.float32
BF16 = jnp.bfloat16
FH = 5
AH = 3
WIN = 7
PER = 128 // WIN
PROF = 120


def swap(block, flip_x, parity):
    nx, ny = lax.axis_size("gx"), lax.axis_size("gy")
    route = []
    for a in range(nx):
        for b in range(ny):
            ta = a ^ 1 if flip_x else a
            tb = b if parity is None else ((b + parity) ^ 1) - parity
            if 0 <= ta < nx and 0 <= tb < ny:
                route.append((a * ny + b, ta * ny + tb))
    return lax.ppermute(block, ("gx", "gy"), route)


FWD, ADJ = ("fe", "fh"), ("ae", "ah")
def side_parts(e, h):
    return [(e, c, i) for c in range(3) for i in range(2)] + [(h, c, i) for c in range(3) for i in range(2)] + [(h, 0, 2), (h, 2, 2)]


CO_RAW, CO_WIN = [("co", 0, i) for i in (0, 1)], [("co", 0, i) for i in (2, 3)]
F_RAW = side_parts(*FWD) + CO_RAW
A_RAW = side_parts(*ADJ)
F_WIN = [("fe", c, i) for c in range(3) for i in (2, 3, 4)] + [("fh", 1, 2)]
F_WIN += [("fh", c, 3) for c in range(3)] + [("fh", 0, 4), ("fh", 2, 4)] + CO_WIN
C_RAW = side_parts(*FWD) + [("fe", 1, 2)] + A_RAW + [("ae", 1, 2)] + CO_RAW
C_WIN = [(n, c, i) for n in FWD for c in range(3) for i in range(FH)] + CO_RAW + CO_WIN


def x_parts(yl):
    raw = [(n, c, y) for n in FWD + ADJ for c in range(3) for y in range(yl)]
    win = [(n, c, y) for n in FWD for c in range(3) for y in range(yl)]
    co = [("co", 0, y) for y in range(yl)]
    return raw + co, win + co


def ceil(a, b):
    return -(-a // b)


def stepped(e, h, out, xl, yl):
    sub = lax.broadcasted_iota(jnp.int32, (xl, 128), 0)
    x_last = sub == xl - 1
    z_last = lax.broadcasted_iota(jnp.int32, (xl, 128), 1) == 127
    zup = lambda v: jnp.where(z_last, 0.0, pltpu.roll(v, 127, 1)) - v
    xup = lambda v: jnp.where(x_last, 0.0, pltpu.roll(v, xl - 1, 0)) - v
    row = lambda ref, c, y: ref[pl.ds(c * xl * yl + y, xl, stride=yl), :]
    cur = [row(e, c, 0) for c in range(3)]
    for y in range(yl - 1):
        up = [row(e, c, y + 1) for c in range(3)]
        ex, ey, ez = cur
        out[0, y] = row(h, 0, y) - DT * ((up[2] - ez) - zup(ey))
        out[1, y] = row(h, 1, y) - DT * (zup(ex) - xup(ez))
        out[2, y] = row(h, 2, y) - DT * (xup(ey) - (up[0] - ex))
        cur = up


def edge_row(e, h, h1, is_h, c, i, up, x, count, xl, yl):
    here = jnp.where(up, yl - 1 - i, i)
    flat = lambda ref, r: ref[pl.ds(c * xl * yl + x * yl + r, count, stride=yl), :]
    if not is_h:
        return flat(e, here)
    if i in (1, 2):
        return h1[c, here, pl.ds(x, count), :]
    return jnp.where(up, flat(h, yl - 1 - i), h1[c, i, pl.ds(x, count), :])


def fetch_body(ae, ah, fe, fh, bg, *rest, xl, yl):
    outs, (h1, aa, ab, sems) = rest[:5], rest[5:]
    copies = [pltpu.make_async_copy(s, d, sems.at[i]) for i, (s, d) in enumerate(zip((ae, ah, fe, fh, bg), outs))]
    for c in copies:
        c.start()
    copies[0].wait()
    copies[1].wait()
    e, h = outs[0], outs[1]
    gy = lax.axis_index("gy")
    stepped(e, h, h1, xl, yl)
    for u, (name, c, i) in enumerate(A_RAW):
        for dst, up in ((aa, gy % 2 == 0), (ab, gy % 2 == 1)):
            dst[u] = edge_row(e, h, h1, name == "ah", c, i, up, 0, xl, xl, yl)
    for c in copies[2:]:
        c.wait()


def first_body(fe, fh, h1, *, xl, yl):
    stepped(fe, fh, h1, xl, yl)


def send_body(mon, fe, fh, ae, ah, bg, fh1, ah1, sp, *rest, xl, yl, nw, owned):
    parts, (co, prof_t, fa, fb, px, da, db, turn) = rest[:nw], rest[nw:]
    gx, gy, w = lax.axis_index("gx"), lax.axis_index("gy"), lax.axis_index("wl")
    plane = xl * yl
    depth = nw * owned
    lane = lax.broadcasted_iota(jnp.int32, (xl, 128), 1)
    lane8 = lane[0:8]
    first = WIN // 2 - mon[0] + 256
    refs = dict(fe=fe, fh=fh, ae=ae, ah=ah)
    turn[...] = jnp.zeros((128, 128), F32)
    for k in range(nw):
        for i in range(owned):
            turn[pl.ds(owned * (w ^ k) + i, yl, stride=depth), 0:xl] = parts[k][i]
    layers = jnp.transpose(turn[...])[0:xl]
    for y in range(yl):
        moved = pltpu.roll(layers, (Z0 - depth * y) % 128, 1)
        perm = jnp.where((lane >= Z0) & (lane < Z0 + depth), moved, bg[pl.ds(y, xl, stride=yl), :])
        co[y] = DT / perm
    turn[0:yl, 0:xl] = sp[...]
    prof_t[...] = jnp.transpose(turn[...])[0:xl]
    low_x = gx == 0
    x8 = pl.multiple_of(jnp.where(low_x, xl - 8, 0), 8)

    def beside(name, c, y, x, count):
        if name == "co":
            return co[y, pl.ds(x, count), :]
        return refs[name][pl.ds(c * plane + x * yl + y, count, stride=yl), :]

    def beyond(up):
        def rows(name, c, i, x, count):
            if name == "co":
                return co[jnp.where(up, yl - 1 - i, i), pl.ds(x, count), :]
            e, h, h1 = (fe, fh, fh1) if name in FWD else (ae, ah, ah1)
            return edge_row(e, h, h1, name in ("fh", "ah"), c, i, up, x, count, xl, yl)
        return rows

    def windows(parts, x, count, rows):
        out = []
        here = lax.broadcasted_iota(jnp.int32, (count, 128), 1)
        for t in range(ceil(len(parts), PER)):
            acc = jnp.zeros((count, 128), F32)
            for q, (name, c, i) in enumerate(parts[t * PER : (t + 1) * PER]):
                moved = pltpu.roll(rows(name, c, i, x, count), (WIN * q + first) % 128, 1)
                acc = jnp.where((here >= WIN * q) & (here < WIN * (q + 1)), moved, acc)
            out.append(acc)
        return out

    def tiles(dst, raw, win, rows):
        for n, (name, c, i) in enumerate(raw):
            half = pltpu.roll(rows(name, c, i, x8, 8), jnp.where(low_x, 4, 0), 0)[0:4]
            dst[n // 2, 4 * (n % 2) : 4 * (n % 2) + 4, :] = half
        at = ceil(len(raw), 2)
        for tile in windows(win, x8, 8, rows):
            dst[at] = tile
            at += 1
        return at

    for dst, corner, up in ((fa, da, gy % 2 == 0), (fb, db, gy % 2 == 1)):
        rows = beyond(up)
        for u, (name, c, i) in enumerate(F_RAW):
            dst[u] = rows(name, c, i, 0, xl)
        at = len(F_RAW)
        for unit in windows(F_WIN, 0, xl, rows):
            dst[at] = unit
            at += 1
        mix = dst[at - 1]
        prof = prof_t[...]
        for i in range(FH):
            col = jnp.where(up, prof[:, yl - 1 - i : yl - i], prof[:, i : i + 1])
            mix = jnp.where(lane == PROF + i, jnp.broadcast_to(col, (xl, 128)), mix)
        dst[at - 1] = mix
        last = tiles(corner, C_RAW, C_WIN, rows)
        src8 = dst[at - 1, pl.ds(x8, 8), :]
        corner[last - 1] = jnp.where((lane8 >= PROF) & (lane8 < PROF + FH), src8, corner[last - 1])
    raw, win = x_parts(yl)
    last = tiles(px, raw, win, beside)
    px[last] = prof_t[pl.ds(x8, 8), :]


class Halo:
    def __init__(self, mon, xl, yl, put):
        self.xl, self.yl, self.put = xl, yl, put
        self.gx, self.gy = lax.axis_index("gx"), lax.axis_index("gy")
        self.back = mon - WIN // 2 + 256
        sub = lax.broadcasted_iota(jnp.int32, (8, 128), 0)
        low = self.gx == 0
        mask = lambda lo, hi: jnp.where(low, lo.astype(F32), hi.astype(F32))
        self.keep = mask(sub < FH, sub >= 8 - FH)
        self.near = mask(sub < 4, sub >= 4) > 0.5
        self.far = mask((sub >= 4) & (sub < FH), (sub < 4) & (sub >= 8 - FH)) > 0.5
        self.shift = [jnp.where(low, 0, 4), jnp.where(low, 4, 0)]

    def row(self, i, high):
        return jnp.where(high, FH + self.yl + i, FH - 1 - i)

    def unroll(self, tile, q):
        return pltpu.roll(tile, (self.back - WIN * q) % 128, 1)

    def side(self, ref, raw, win, high):
        own = pl.ds(0, self.xl)
        for u, (name, c, i) in enumerate(raw):
            self.put(name, c, self.row(i, high), own, ref[u])
        for s, (name, c, i) in enumerate(win):
            self.put(name, c, self.row(i, high), own, self.unroll(ref[len(raw) + s // PER], s % PER))

    def tiles(self, ref, raw, win, names, where):
        halo = pl.ds(self.xl, 8)
        seats = {part: s for s, part in enumerate(win)}
        at = ceil(len(raw), 2)
        for n, part in enumerate(raw):
            if part[0] not in names:
                continue
            value = jnp.where(self.near, pltpu.roll(ref[n // 2], self.shift[n % 2], 0), 0.0)
            if part in seats:
                s = seats.pop(part)
                value = jnp.where(self.far, self.unroll(ref[at + s // PER], s % PER), value)
            self.put(part[0], part[1], where(part[2]), halo, value)
        for part, s in seats.items():
            if part[0] in names:
                self.put(part[0], part[1], where(part[2]), halo, self.unroll(ref[at + s // PER], s % PER) * self.keep)


class Stepper:
    def __init__(self, xl, yl, cx):
        self.xr = xr = xl + 8
        self.cx = cx
        gx, gy = lax.axis_index("gx"), lax.axis_index("gy")
        self.lane = lax.broadcasted_iota(jnp.int32, (xr, 128), 1)
        ring = lax.broadcasted_iota(jnp.int32, (xr, 128), 0)
        inside_low = jnp.where(ring < xl + FH, F32(DT), F32(0.0))
        inside_high = jnp.where((ring < xl) | (ring >= xr - FH), F32(DT), F32(0.0))
        self.h_in = jnp.where(gx == 0, inside_low, inside_high)
        self.h_low = self.h_in * jnp.where(gy == 0, 0.0, 1.0).astype(F32)
        edge = ((ring == xl - 1) | (ring == xr - 1)).astype(F32)
        self.h_edge = self.h_in * edge
        self.z_last = self.lane == 127
        ri = lax.broadcasted_iota(jnp.int32, (128, 128), 0)
        ci = lax.broadcasted_iota(jnp.int32, (128, 128), 1)
        diff = jnp.where(ri == ci, F32(1.0), F32(0.0)) - jnp.where(ri == ci - 1, F32(1.0), F32(0.0))
        self.diff = jnp.concatenate([diff] * 3, 0).astype(BF16)

    def zdn(self, p, q):
        v = jnp.concatenate([p, q], 0)
        hi = v.astype(BF16)
        rest = v - hi.astype(F32)
        mid = rest.astype(BF16)
        low = (rest - mid.astype(F32)).astype(BF16)
        out = lax.dot_general(jnp.concatenate([hi, mid, low], 1), self.diff, (((1,), (0,)), ((), ())),
                              preferred_element_type=F32)
        return out[0 : self.xr], out[self.xr :]

    def zup(self, v):
        return jnp.where(self.z_last, 0.0, pltpu.roll(v, 127, 1)) - v

    def xup(self, v):
        return pltpu.roll(v, self.xr - 1, 0) - v

    def xdn(self, v):
        return v - pltpu.roll(v, 1, 0)

    def rows(self, e, h, start, stop, given=()):
        load = lambda ref, y: (ref[0, y], ref[1, y], ref[2, y])
        cur, now = load(e, start), None
        for y in range(start, stop):
            up = load(e, y + 1)
            below = now
            k = self.h_low if y < FH else self.h_in
            ex, ey, ez = cur
            if y in given:
                k = self.h_edge
                now = (
                    h[0, y],
                    h[1, y] + k * pltpu.roll(ez, self.xr - 1, 0),
                    h[2, y] - k * pltpu.roll(ey, self.xr - 1, 0),
                )
            else:
                now = (
                    h[0, y] - k * ((up[2] - ez) - self.zup(ey)),
                    h[1, y] - k * (self.zup(ex) - self.xup(ez)),
                    h[2, y] - k * (self.xup(ey) - (up[0] - ex)),
                )
            for c in range(3):
                h[c, y] = now[c]
            if y > start:
                hx, hy, hz = now
                k = self.cx[y]
                zy, zx = self.zdn(hy, hx)
                yield y, cur, (
                    k * ((hz - below[2]) - zy),
                    k * (zx - self.xdn(hz)),
                    k * (self.xdn(hy) - (hx - below[0])),
                )
            cur = up


def given_rows(yl):
    return {FH - 3, FH - 2, *range(FH + yl, yl + 2 * FH)}


def pick(values):
    w = lax.axis_index("wl")
    value = F32(values[0])
    for i in range(1, len(values)):
        value = jnp.where(w == i, F32(values[i]), value)
    return value


def fill_own(refs, bigs, xl, yl):
    for ref, big in zip(refs, bigs):
        for c in range(3):
            for y in range(yl):
                big[c, FH + y, 0:xl, :] = ref[pl.ds(c * xl * yl + y, xl, stride=yl), :]


def put_out(big, out, xl, yl):
    for c in range(3):
        for y in range(yl):
            out[pl.ds(c * xl * yl + y, xl, stride=yl), :] = big[c, FH + y, 0:xl, :]


def store_body(e3, a, out_f, out_a, *, xl, yl):
    put_out(e3, out_f, xl, yl)
    put_out(a, out_a, xl, yl)


def forward_body(src, mon, fe, fh, co, prof_t, ra, rb, rx, rda, rdb, cx, e1, e2, e3, e0, h, sx, *, xl, yl, signals):
    xr, yr = xl + 8, yl + 2 * FH
    gy = lax.axis_index("gy")
    src_l = src[0]
    own, halo = pl.ds(0, xl), pl.ds(xl, 8)

    def put(name, c, row, cols, value):
        if name == "co":
            cx[row, cols, :] = value
        else:
            (e0 if name == "fe" else h)[c, row, cols, :] = value

    to = Halo(mon[0], xl, yl, put)
    fill_own((fe, fh), (e0, h), xl, yl)
    for y in range(yl):
        cx[FH + y, own, :] = co[y]
    names = FWD + ("co",)
    raw, win = x_parts(yl)
    to.tiles(rx, raw, win, names, lambda y: FH + y)
    at_src = lax.broadcasted_iota(jnp.int32, (xl, 128), 1) == src_l
    at_src8 = lax.broadcasted_iota(jnp.int32, (8, 128), 1) == src_l

    def source(row, wide, tile, lane):
        sx[row, own, :] = jnp.where(at_src, jnp.broadcast_to(wide[:, lane : lane + 1], (xl, 128)), 0.0)
        sx[row, halo, :] = jnp.where(at_src8, jnp.broadcast_to(tile[:, lane : lane + 1], (8, 128)), 0.0)

    prof, prof_x = prof_t[...], rx[rx.shape[0] - 1] * to.keep
    for y in range(yl):
        source(FH + y, prof, prof_x, y)
    for ref, ref_d, high in ((ra, rda, gy % 2 == 0), (rb, rdb, gy % 2 == 1)):
        to.side(ref, F_RAW, F_WIN, high)
        to.tiles(ref_d, C_RAW, C_WIN, names, lambda i, high=high: to.row(i, high))
        prof_y, prof_d = ref[ref.shape[0] - 1], ref_d[ref_d.shape[0] - 1] * to.keep
        for i in range(FH):
            source(to.row(i, high), prof_y, prof_d, PROF + i)
    step = Stepper(xl, yl, cx)
    runs = (e0, e1, e2, e3)
    for k in range(STEPS):
        new = runs[k + 1]
        signal = pick([s[k] for s in signals])
        for y, cur, inc in step.rows(runs[k], h, k, yr - 1 - k, given_rows(yl) if k == 0 else ()):
            new[0, y] = cur[0] + inc[0] + signal * sx[y]
            new[1, y] = cur[1] + inc[1]
            new[2, y] = cur[2] + inc[2]


def adjoint_body(mon, ae, ah, cx, e1, e2, e3, ra, rb, rx, rda, rdb, a, grad, g, *, xl, yl, omegas):
    yr = yl + 2 * FH
    gy = lax.axis_index("gy")

    def put(name, c, row, cols, value):
        (a if name == "ae" else g)[c, row, cols, :] = value

    to = Halo(mon[0], xl, yl, put)
    for c in range(3):
        a[c, FH - AH] = jnp.zeros((xl + 8, 128), F32)
    fill_own((ae, ah), (a, g), xl, yl)
    raw, win = x_parts(yl)
    to.tiles(rx, raw, win, ADJ, lambda y: FH + y)
    for ref, ref_d, high in ((ra, rda, gy % 2 == 0), (rb, rdb, gy % 2 == 1)):
        to.side(ref, A_RAW, [], high)
        to.tiles(ref_d, C_RAW, C_WIN, ADJ, lambda i, high=high: to.row(i, high))
    step = Stepper(xl, yl, cx)
    at_mon = step.lane == mon[0]
    total = [None] * yl
    for j in range(STEPS):
        seen = (e3, e2, e1)[j]
        for y, cur, inc in step.rows(a, g, FH - AH + j, yr - AH - j, given_rows(yl) if j == 0 else ()):
            for c in range(3):
                f = seen[c, y]
                v = cur[c] + inc[c] + jnp.where(at_mon, 2.0 * DT * f, 0.0)
                a[c, y] = v
                if FH <= y < FH + yl:
                    t = (f * v)[0:xl]
                    i = y - FH
                    total[i] = t if total[i] is None else total[i] + t
    scale = pick([o * o for o in omegas])
    lane = step.lane[0:xl]
    packed = jnp.zeros((xl, 128), F32)
    wide = 128 // yl
    for y in range(yl):
        moved = pltpu.roll(total[y] * scale, (wide * y - Z0) % 128, 1)
        packed = jnp.where((lane >= wide * y) & (lane < wide * (y + 1)), moved, packed)
    grad[...] = packed


def sum_body(*refs, owned, xl, yl):
    *parts, out, turn = refs
    w = lax.axis_index("wl")
    acc = parts[0][...]
    for p in parts[1:]:
        acc = acc + p[...]
    turn[...] = jnp.transpose(acc)
    for i in range(owned):
        out[i] = turn[pl.ds(owned * w + i, yl, stride=128 // yl), :]


def per_device(fe, fh, ae, ah, background, design, source_profile, source_layer, monitor_layer):
    _, _, xl, yl, nz = fe.shape
    nw = lax.axis_size("wl")
    owned = design.shape[0]
    xr, yr = xl + 8, yl + 2 * FH
    flat = [v.reshape(3 * xl * yl, nz) for v in (fe, fh, ae, ah)] + [background.reshape(xl * yl, nz)]
    sp = jnp.transpose(source_profile[0])
    shape = lambda *s: jax.ShapeDtypeStruct(s, F32)
    smem = pl.BlockSpec(memory_space=pltpu.SMEM)
    vmem = pl.BlockSpec(memory_space=pltpu.VMEM)
    hbm = pl.BlockSpec(memory_space=pltpu.HBM)
    ext = lambda *s: pltpu.VMEM(s, F32)
    field = (3, yr, xr, nz)

    def call(body, name, out, specs, scratch=()):
        return pl.pallas_call(
            body, out_shape=tuple(shape(*s) for s in out), in_specs=specs, out_specs=(vmem,) * len(out),
            scratch_shapes=list(scratch), name=name,
            compiler_params=pltpu.CompilerParams(vmem_limit_bytes=20 * 1024 * 1024),
        )

    def over_wl(v):
        return [v] + [lax.ppermute(v, "wl", [(i, i ^ k) for i in range(nw)]) for k in range(1, nw)]

    raw, win = x_parts(yl)
    f_side = (len(F_RAW) + ceil(len(F_WIN), PER), xl, nz)
    a_side = (len(A_RAW), xl, nz)
    corner = (ceil(len(C_RAW), 2) + ceil(len(C_WIN), PER), 8, nz)
    beside = (ceil(len(raw), 2) + ceil(len(win), PER) + 1, 8, nz)

    layers = over_wl(jnp.transpose(design, (0, 2, 1)))
    fe, fh, ae, ah, bg = flat
    h1 = (3, yl, xl, nz)
    ae, ah, fe, fh, bg, ah1, aa, ab = call(
        lambda *r: fetch_body(*r, xl=xl, yl=yl), "fetch",
        [ae.shape] * 4 + [bg.shape, h1, a_side, a_side], [hbm] * 5, [pltpu.SemaphoreType.DMA((5,))],
    )(*[pltpu.with_memory_space_constraint(v, pltpu.HBM) for v in (ae, ah, fe, fh, bg)])
    raa, rab = swap(aa, False, 0), swap(ab, False, 1)
    (fh1,) = call(lambda *r: first_body(*r, xl=xl, yl=yl), "first", [h1], [vmem] * 2)(fe, fh)
    co, prof_t, fa, fb, px, da, db = call(
        lambda *r: send_body(*r, xl=xl, yl=yl, nw=nw, owned=owned), "send",
        [(yl, xl, nz), (xl, nz), f_side, f_side, beside, corner, corner],
        [smem] + [vmem] * (8 + nw), [ext(128, 128)],
    )(monitor_layer, fe, fh, ae, ah, bg, fh1, ah1, sp, *layers)
    rfa, rfb = swap(fa, False, 0), swap(fb, False, 1)
    rx = swap(px, True, None)
    rda, rdb = swap(da, True, 0), swap(db, True, 1)
    f32 = np.float32
    omegas = [f32(2.0 * math.pi) / (f32(16.0) + f32(32.0) * f32(i) / f32(nw)) for i in range(nw)]
    signals = [[f32(DT) * np.sin(f32(o * f32((k + 1) * DT))) for k in range(STEPS)] for o in omegas]
    cx, e1, e2, e3 = call(
        lambda *r: forward_body(*r, xl=xl, yl=yl, signals=signals), "forward",
        [(yr, xr, nz), field, field, field], [smem, smem] + [vmem] * 9,
        [ext(*field), ext(*field), ext(yr, xr, nz)],
    )(source_layer, monitor_layer, fe, fh, co, prof_t, rfa, rfb, rx, rda, rdb)
    last_a, grad = call(
        lambda *r: adjoint_body(*r, xl=xl, yl=yl, omegas=omegas), "adjoint",
        [field, (xl, nz)], [smem] + [vmem] * 11, [ext(*field)],
    )(monitor_layer, ae, ah, cx, e1, e2, e3, raa, rab, rx, rda, rdb)
    terms = over_wl(grad)
    out_f, out_a = call(
        lambda *r: store_body(*r, xl=xl, yl=yl), "store", [flat[0].shape] * 2, [vmem] * 2)(e3, last_a)
    (gradient,) = call(
        lambda *r: sum_body(*r, owned=owned, xl=xl, yl=yl), "gather_sum",
        [(owned, yl, xl)], [vmem] * nw, [ext(128, xl)],
    )(*terms)
    block = (1, 3, xl, yl, nz)
    return (out_f.reshape(block), out_a.reshape(block), jnp.transpose(gradient, (0, 2, 1)))


def solution(mesh):
    field = P("wl", None, "gx", "gy", None)
    return jax.shard_map(
        per_device,
        mesh=mesh,
        in_specs=(field, field, field, field, P("gx", "gy", None), P("wl", "gx", "gy"),
                  P("wl", "gx", "gy"), P("wl"), P("wl")),
        out_specs=(field, field, P("wl", "gx", "gy")),
        check_vma=False,
    )
```

```python
import math

import jax
import jax.numpy as jnp
import numpy as np
from jax import lax
from jax.experimental import pallas as pl
from jax.experimental.pallas import tpu as pltpu
from jax.sharding import PartitionSpec as P

Z0 = 64
STEPS = 3
DT = 0.5
F32 = jnp.float32
BF16 = jnp.bfloat16
FH = 5
AH = 3
WIN = 7
PER = 128 // WIN
PROF = 120


def swap(block, flip_x, parity):
    nx, ny = lax.axis_size("gx"), lax.axis_size("gy")
    route = []
    for a in range(nx):
        for b in range(ny):
            ta = a ^ 1 if flip_x else a
            tb = b if parity is None else ((b + parity) ^ 1) - parity
            if 0 <= ta < nx and 0 <= tb < ny:
                route.append((a * ny + b, ta * ny + tb))
    return lax.ppermute(block, ("gx", "gy"), route)


FWD, ADJ = ("fe", "fh"), ("ae", "ah")
def side_parts(e, h):
    return [(e, c, i) for c in range(3) for i in range(2)] + [(h, c, i) for c in range(3) for i in range(2)] + [(h, 0, 2), (h, 2, 2)]


CO_RAW, CO_WIN = [("co", 0, i) for i in (0, 1)], [("co", 0, i) for i in (2, 3)]
F_RAW = side_parts(*FWD) + CO_RAW
A_RAW = side_parts(*ADJ)
F_WIN = [("fe", c, i) for c in range(3) for i in (2, 3, 4)] + [("fh", 1, 2)]
F_WIN += [("fh", c, 3) for c in range(3)] + [("fh", 0, 4), ("fh", 2, 4)] + CO_WIN
C_RAW = side_parts(*FWD) + [("fe", 1, 2)] + A_RAW + [("ae", 1, 2)] + CO_RAW
C_WIN = [(n, c, i) for n in FWD for c in range(3) for i in range(FH)] + CO_RAW + CO_WIN


def x_parts(yl):
    raw = [(n, c, y) for n in FWD + ADJ for c in range(3) for y in range(yl)]
    win = [(n, c, y) for n in FWD for c in range(3) for y in range(yl)]
    co = [("co", 0, y) for y in range(yl)]
    return raw + co, win + co


def ceil(a, b):
    return -(-a // b)


def stepped(e, h, out, xl, yl):
    sub = lax.broadcasted_iota(jnp.int32, (xl, 128), 0)
    x_last = sub == xl - 1
    z_last = lax.broadcasted_iota(jnp.int32, (xl, 128), 1) == 127
    zup = lambda v: jnp.where(z_last, 0.0, pltpu.roll(v, 127, 1)) - v
    xup = lambda v: jnp.where(x_last, 0.0, pltpu.roll(v, xl - 1, 0)) - v
    row = lambda ref, c, y: ref[pl.ds(c * xl * yl + y, xl, stride=yl), :]
    cur = [row(e, c, 0) for c in range(3)]
    for y in range(yl - 1):
        up = [row(e, c, y + 1) for c in range(3)]
        ex, ey, ez = cur
        out[0, y] = row(h, 0, y) - DT * ((up[2] - ez) - zup(ey))
        out[1, y] = row(h, 1, y) - DT * (zup(ex) - xup(ez))
        out[2, y] = row(h, 2, y) - DT * (xup(ey) - (up[0] - ex))
        cur = up


def edge_row(e, h, h1, is_h, c, i, up, x, count, xl, yl):
    here = jnp.where(up, yl - 1 - i, i)
    flat = lambda ref, r: ref[pl.ds(c * xl * yl + x * yl + r, count, stride=yl), :]
    if not is_h:
        return flat(e, here)
    if i in (1, 2):
        return h1[c, here, pl.ds(x, count), :]
    return jnp.where(up, flat(h, yl - 1 - i), h1[c, i, pl.ds(x, count), :])


def fetch_body(ae, ah, fe, fh, bg, *rest, xl, yl):
    outs, (h1, fh1, aa, ab, sems) = rest[:5], rest[5:]
    copies = [pltpu.make_async_copy(s, d, sems.at[i]) for i, (s, d) in enumerate(zip((ae, ah, fe, fh, bg), outs))]
    for c in copies:
        c.start()
    copies[0].wait()
    copies[1].wait()
    e, h = outs[0], outs[1]
    gy = lax.axis_index("gy")
    stepped(e, h, h1, xl, yl)
    for u, (name, c, i) in enumerate(A_RAW):
        for dst, up in ((aa, gy % 2 == 0), (ab, gy % 2 == 1)):
            dst[u] = edge_row(e, h, h1, name == "ah", c, i, up, 0, xl, xl, yl)
    copies[2].wait()
    copies[3].wait()
    stepped(outs[2], outs[3], fh1, xl, yl)
    copies[4].wait()


def send_body(mon, fe, fh, ae, ah, bg, fh1, ah1, sp, *rest, xl, yl, nw, owned):
    parts, (co, prof_t, fa, fb, px, da, db, turn) = rest[:nw], rest[nw:]
    gx, gy, w = lax.axis_index("gx"), lax.axis_index("gy"), lax.axis_index("wl")
    plane = xl * yl
    depth = nw * owned
    lane = lax.broadcasted_iota(jnp.int32, (xl, 128), 1)
    lane8 = lane[0:8]
    first = WIN // 2 - mon[0] + 256
    refs = dict(fe=fe, fh=fh, ae=ae, ah=ah)
    turn[...] = jnp.zeros((128, 128), F32)
    for k in range(nw):
        for i in range(owned):
            turn[pl.ds(owned * (w ^ k) + i, yl, stride=depth), 0:xl] = parts[k][i]
    layers = jnp.transpose(turn[...])[0:xl]
    for y in range(yl):
        moved = pltpu.roll(layers, (Z0 - depth * y) % 128, 1)
        perm = jnp.where((lane >= Z0) & (lane < Z0 + depth), moved, bg[pl.ds(y, xl, stride=yl), :])
        co[y] = DT / perm
    turn[0:yl, 0:xl] = sp[...]
    prof_t[...] = jnp.transpose(turn[...])[0:xl]
    low_x = gx == 0
    x8 = pl.multiple_of(jnp.where(low_x, xl - 8, 0), 8)

    def beside(name, c, y, x, count):
        if name == "co":
            return co[y, pl.ds(x, count), :]
        return refs[name][pl.ds(c * plane + x * yl + y, count, stride=yl), :]

    def beyond(up):
        def rows(name, c, i, x, count):
            if name == "co":
                return co[jnp.where(up, yl - 1 - i, i), pl.ds(x, count), :]
            e, h, h1 = (fe, fh, fh1) if name in FWD else (ae, ah, ah1)
            return edge_row(e, h, h1, name in ("fh", "ah"), c, i, up, x, count, xl, yl)
        return rows

    def windows(parts, x, count, rows):
        out = []
        here = lax.broadcasted_iota(jnp.int32, (count, 128), 1)
        for t in range(ceil(len(parts), PER)):
            acc = jnp.zeros((count, 128), F32)
            for q, (name, c, i) in enumerate(parts[t * PER : (t + 1) * PER]):
                moved = pltpu.roll(rows(name, c, i, x, count), (WIN * q + first) % 128, 1)
                acc = jnp.where((here >= WIN * q) & (here < WIN * (q + 1)), moved, acc)
            out.append(acc)
        return out

    def tiles(dst, raw, win, rows):
        for n, (name, c, i) in enumerate(raw):
            half = pltpu.roll(rows(name, c, i, x8, 8), jnp.where(low_x, 4, 0), 0)[0:4]
            dst[n // 2, 4 * (n % 2) : 4 * (n % 2) + 4, :] = half
        at = ceil(len(raw), 2)
        for tile in windows(win, x8, 8, rows):
            dst[at] = tile
            at += 1
        return at

    for dst, corner, up in ((fa, da, gy % 2 == 0), (fb, db, gy % 2 == 1)):
        rows = beyond(up)
        for u, (name, c, i) in enumerate(F_RAW):
            dst[u] = rows(name, c, i, 0, xl)
        at = len(F_RAW)
        for unit in windows(F_WIN, 0, xl, rows):
            dst[at] = unit
            at += 1
        mix = dst[at - 1]
        prof = prof_t[...]
        for i in range(FH):
            col = jnp.where(up, prof[:, yl - 1 - i : yl - i], prof[:, i : i + 1])
            mix = jnp.where(lane == PROF + i, jnp.broadcast_to(col, (xl, 128)), mix)
        dst[at - 1] = mix
        last = tiles(corner, C_RAW, C_WIN, rows)
        src8 = dst[at - 1, pl.ds(x8, 8), :]
        corner[last - 1] = jnp.where((lane8 >= PROF) & (lane8 < PROF + FH), src8, corner[last - 1])
    raw, win = x_parts(yl)
    last = tiles(px, raw, win, beside)
    px[last] = prof_t[pl.ds(x8, 8), :]


class Halo:
    def __init__(self, mon, xl, yl, put):
        self.xl, self.yl, self.put = xl, yl, put
        self.gx, self.gy = lax.axis_index("gx"), lax.axis_index("gy")
        self.back = mon - WIN // 2 + 256
        sub = lax.broadcasted_iota(jnp.int32, (8, 128), 0)
        low = self.gx == 0
        mask = lambda lo, hi: jnp.where(low, lo.astype(F32), hi.astype(F32))
        self.keep = mask(sub < FH, sub >= 8 - FH)
        self.near = mask(sub < 4, sub >= 4) > 0.5
        self.far = mask((sub >= 4) & (sub < FH), (sub < 4) & (sub >= 8 - FH)) > 0.5
        self.shift = [jnp.where(low, 0, 4), jnp.where(low, 4, 0)]

    def row(self, i, high):
        return jnp.where(high, FH + self.yl + i, FH - 1 - i)

    def unroll(self, tile, q):
        return pltpu.roll(tile, (self.back - WIN * q) % 128, 1)

    def side(self, ref, raw, win, high):
        own = pl.ds(0, self.xl)
        for u, (name, c, i) in enumerate(raw):
            self.put(name, c, self.row(i, high), own, ref[u])
        for s, (name, c, i) in enumerate(win):
            self.put(name, c, self.row(i, high), own, self.unroll(ref[len(raw) + s // PER], s % PER))

    def tiles(self, ref, raw, win, names, where):
        halo = pl.ds(self.xl, 8)
        seats = {part: s for s, part in enumerate(win)}
        at = ceil(len(raw), 2)
        for n, part in enumerate(raw):
            if part[0] not in names:
                continue
            value = jnp.where(self.near, pltpu.roll(ref[n // 2], self.shift[n % 2], 0), 0.0)
            if part in seats:
                s = seats.pop(part)
                value = jnp.where(self.far, self.unroll(ref[at + s // PER], s % PER), value)
            self.put(part[0], part[1], where(part[2]), halo, value)
        for part, s in seats.items():
            if part[0] in names:
                self.put(part[0], part[1], where(part[2]), halo, self.unroll(ref[at + s // PER], s % PER) * self.keep)


class Stepper:
    def __init__(self, xl, yl, cx):
        self.xr = xr = xl + 8
        self.cx = cx
        gx, gy = lax.axis_index("gx"), lax.axis_index("gy")
        self.lane = lax.broadcasted_iota(jnp.int32, (xr, 128), 1)
        ring = lax.broadcasted_iota(jnp.int32, (xr, 128), 0)
        inside_low = jnp.where(ring < xl + FH, F32(DT), F32(0.0))
        inside_high = jnp.where((ring < xl) | (ring >= xr - FH), F32(DT), F32(0.0))
        self.h_in = jnp.where(gx == 0, inside_low, inside_high)
        self.h_low = self.h_in * jnp.where(gy == 0, 0.0, 1.0).astype(F32)
        edge = ((ring == xl - 1) | (ring == xr - 1)).astype(F32)
        self.h_edge = self.h_in * edge
        self.z_last = self.lane == 127
        ri = lax.broadcasted_iota(jnp.int32, (128, 128), 0)
        ci = lax.broadcasted_iota(jnp.int32, (128, 128), 1)
        diff = jnp.where(ri == ci, F32(1.0), F32(0.0)) - jnp.where(ri == ci - 1, F32(1.0), F32(0.0))
        self.diff = jnp.concatenate([diff] * 3, 0).astype(BF16)

    def zdn(self, p, q):
        v = jnp.concatenate([p, q], 0)
        hi = v.astype(BF16)
        rest = v - hi.astype(F32)
        mid = rest.astype(BF16)
        low = (rest - mid.astype(F32)).astype(BF16)
        out = lax.dot_general(jnp.concatenate([hi, mid, low], 1), self.diff, (((1,), (0,)), ((), ())),
                              preferred_element_type=F32)
        return out[0 : self.xr], out[self.xr :]

    def zup(self, v):
        return jnp.where(self.z_last, 0.0, pltpu.roll(v, 127, 1)) - v

    def xup(self, v):
        return pltpu.roll(v, self.xr - 1, 0) - v

    def xdn(self, v):
        return v - pltpu.roll(v, 1, 0)

    def rows(self, e, h, start, stop, given=()):
        load = lambda ref, y: (ref[0, y], ref[1, y], ref[2, y])
        cur, now = load(e, start), None
        for y in range(start, stop):
            up = load(e, y + 1)
            below = now
            k = self.h_low if y < FH else self.h_in
            ex, ey, ez = cur
            if y in given:
                k = self.h_edge
                now = (
                    h[0, y],
                    h[1, y] + k * pltpu.roll(ez, self.xr - 1, 0),
                    h[2, y] - k * pltpu.roll(ey, self.xr - 1, 0),
                )
            else:
                now = (
                    h[0, y] - k * ((up[2] - ez) - self.zup(ey)),
                    h[1, y] - k * (self.zup(ex) - self.xup(ez)),
                    h[2, y] - k * (self.xup(ey) - (up[0] - ex)),
                )
            for c in range(3):
                h[c, y] = now[c]
            if y > start:
                hx, hy, hz = now
                k = self.cx[y]
                zy, zx = self.zdn(hy, hx)
                yield y, cur, (
                    k * ((hz - below[2]) - zy),
                    k * (zx - self.xdn(hz)),
                    k * (self.xdn(hy) - (hx - below[0])),
                )
            cur = up


def given_rows(yl):
    return {FH - 3, FH - 2, *range(FH + yl, yl + 2 * FH)}


def pick(values):
    w = lax.axis_index("wl")
    value = F32(values[0])
    for i in range(1, len(values)):
        value = jnp.where(w == i, F32(values[i]), value)
    return value


def fill_own(refs, bigs, xl, yl):
    for ref, big in zip(refs, bigs):
        for c in range(3):
            for y in range(yl):
                big[c, FH + y, 0:xl, :] = ref[pl.ds(c * xl * yl + y, xl, stride=yl), :]


def put_out(big, out, xl, yl):
    for c in range(3):
        for y in range(yl):
            out[pl.ds(c * xl * yl + y, xl, stride=yl), :] = big[c, FH + y, 0:xl, :]


def store_body(e3, a, out_f, out_a, *, xl, yl):
    put_out(e3, out_f, xl, yl)
    put_out(a, out_a, xl, yl)


def forward_body(src, mon, fe, fh, co, prof_t, ra, rb, rx, rda, rdb, cx, e1, e2, e3, e0, h, sx, *, xl, yl, signals):
    xr, yr = xl + 8, yl + 2 * FH
    gy = lax.axis_index("gy")
    src_l = src[0]
    own, halo = pl.ds(0, xl), pl.ds(xl, 8)

    def put(name, c, row, cols, value):
        if name == "co":
            cx[row, cols, :] = value
        else:
            (e0 if name == "fe" else h)[c, row, cols, :] = value

    to = Halo(mon[0], xl, yl, put)
    fill_own((fe, fh), (e0, h), xl, yl)
    for y in range(yl):
        cx[FH + y, own, :] = co[y]
    names = FWD + ("co",)
    raw, win = x_parts(yl)
    to.tiles(rx, raw, win, names, lambda y: FH + y)
    at_src = lax.broadcasted_iota(jnp.int32, (xl, 128), 1) == src_l
    at_src8 = lax.broadcasted_iota(jnp.int32, (8, 128), 1) == src_l

    def source(row, wide, tile, lane):
        sx[row, own, :] = jnp.where(at_src, jnp.broadcast_to(wide[:, lane : lane + 1], (xl, 128)), 0.0)
        sx[row, halo, :] = jnp.where(at_src8, jnp.broadcast_to(tile[:, lane : lane + 1], (8, 128)), 0.0)

    prof, prof_x = prof_t[...], rx[rx.shape[0] - 1] * to.keep
    for y in range(yl):
        source(FH + y, prof, prof_x, y)
    for ref, ref_d, high in ((ra, rda, gy % 2 == 0), (rb, rdb, gy % 2 == 1)):
        to.side(ref, F_RAW, F_WIN, high)
        to.tiles(ref_d, C_RAW, C_WIN, names, lambda i, high=high: to.row(i, high))
        prof_y, prof_d = ref[ref.shape[0] - 1], ref_d[ref_d.shape[0] - 1] * to.keep
        for i in range(FH):
            source(to.row(i, high), prof_y, prof_d, PROF + i)
    step = Stepper(xl, yl, cx)
    runs = (e0, e1, e2, e3)
    for k in range(STEPS):
        new = runs[k + 1]
        signal = pick([s[k] for s in signals])
        for y, cur, inc in step.rows(runs[k], h, k, yr - 1 - k, given_rows(yl) if k == 0 else ()):
            new[0, y] = cur[0] + inc[0] + signal * sx[y]
            new[1, y] = cur[1] + inc[1]
            new[2, y] = cur[2] + inc[2]


def adjoint_body(mon, ae, ah, cx, e1, e2, e3, ra, rb, rx, rda, rdb, a, grad, g, *, xl, yl, omegas):
    yr = yl + 2 * FH
    gy = lax.axis_index("gy")

    def put(name, c, row, cols, value):
        (a if name == "ae" else g)[c, row, cols, :] = value

    to = Halo(mon[0], xl, yl, put)
    for c in range(3):
        a[c, FH - AH] = jnp.zeros((xl + 8, 128), F32)
    fill_own((ae, ah), (a, g), xl, yl)
    raw, win = x_parts(yl)
    to.tiles(rx, raw, win, ADJ, lambda y: FH + y)
    for ref, ref_d, high in ((ra, rda, gy % 2 == 0), (rb, rdb, gy % 2 == 1)):
        to.side(ref, A_RAW, [], high)
        to.tiles(ref_d, C_RAW, C_WIN, ADJ, lambda i, high=high: to.row(i, high))
    step = Stepper(xl, yl, cx)
    at_mon = step.lane == mon[0]
    total = [None] * yl
    for j in range(STEPS):
        seen = (e3, e2, e1)[j]
        for y, cur, inc in step.rows(a, g, FH - AH + j, yr - AH - j, given_rows(yl) if j == 0 else ()):
            for c in range(3):
                f = seen[c, y]
                v = cur[c] + inc[c] + jnp.where(at_mon, 2.0 * DT * f, 0.0)
                a[c, y] = v
                if FH <= y < FH + yl:
                    t = (f * v)[0:xl]
                    i = y - FH
                    total[i] = t if total[i] is None else total[i] + t
    scale = pick([o * o for o in omegas])
    lane = step.lane[0:xl]
    packed = jnp.zeros((xl, 128), F32)
    wide = 128 // yl
    for y in range(yl):
        moved = pltpu.roll(total[y] * scale, (wide * y - Z0) % 128, 1)
        packed = jnp.where((lane >= wide * y) & (lane < wide * (y + 1)), moved, packed)
    grad[...] = packed


def sum_body(*refs, owned, xl, yl):
    *parts, out, turn = refs
    w = lax.axis_index("wl")
    acc = parts[0][...]
    for p in parts[1:]:
        acc = acc + p[...]
    turn[...] = jnp.transpose(acc)
    for i in range(owned):
        out[i] = turn[pl.ds(owned * w + i, yl, stride=128 // yl), :]


def per_device(fe, fh, ae, ah, background, design, source_profile, source_layer, monitor_layer):
    _, _, xl, yl, nz = fe.shape
    nw = lax.axis_size("wl")
    owned = design.shape[0]
    xr, yr = xl + 8, yl + 2 * FH
    flat = [v.reshape(3 * xl * yl, nz) for v in (fe, fh, ae, ah)] + [background.reshape(xl * yl, nz)]
    sp = jnp.transpose(source_profile[0])
    shape = lambda *s: jax.ShapeDtypeStruct(s, F32)
    smem = pl.BlockSpec(memory_space=pltpu.SMEM)
    vmem = pl.BlockSpec(memory_space=pltpu.VMEM)
    hbm = pl.BlockSpec(memory_space=pltpu.HBM)
    ext = lambda *s: pltpu.VMEM(s, F32)
    field = (3, yr, xr, nz)

    def call(body, name, out, specs, scratch=()):
        return pl.pallas_call(
            body, out_shape=tuple(shape(*s) for s in out), in_specs=specs, out_specs=(vmem,) * len(out),
            scratch_shapes=list(scratch), name=name,
            compiler_params=pltpu.CompilerParams(vmem_limit_bytes=20 * 1024 * 1024),
        )

    def over_wl(v):
        return [v] + [lax.ppermute(v, "wl", [(i, i ^ k) for i in range(nw)]) for k in range(1, nw)]

    raw, win = x_parts(yl)
    f_side = (len(F_RAW) + ceil(len(F_WIN), PER), xl, nz)
    a_side = (len(A_RAW), xl, nz)
    corner = (ceil(len(C_RAW), 2) + ceil(len(C_WIN), PER), 8, nz)
    beside = (ceil(len(raw), 2) + ceil(len(win), PER) + 1, 8, nz)

    layers = over_wl(jnp.transpose(design, (0, 2, 1)))
    fe, fh, ae, ah, bg = flat
    h1 = (3, yl, xl, nz)
    ae, ah, fe, fh, bg, ah1, fh1, aa, ab = call(
        lambda *r: fetch_body(*r, xl=xl, yl=yl), "fetch",
        [ae.shape] * 4 + [bg.shape, h1, h1, a_side, a_side], [hbm] * 5, [pltpu.SemaphoreType.DMA((5,))],
    )(*[pltpu.with_memory_space_constraint(v, pltpu.HBM) for v in (ae, ah, fe, fh, bg)])
    raa, rab = swap(aa, False, 0), swap(ab, False, 1)
    co, prof_t, fa, fb, px, da, db = call(
        lambda *r: send_body(*r, xl=xl, yl=yl, nw=nw, owned=owned), "send",
        [(yl, xl, nz), (xl, nz), f_side, f_side, beside, corner, corner],
        [smem] + [vmem] * (8 + nw), [ext(128, 128)],
    )(monitor_layer, fe, fh, ae, ah, bg, fh1, ah1, sp, *layers)
    rfa, rfb = swap(fa, False, 0), swap(fb, False, 1)
    rx = swap(px, True, None)
    rda, rdb = swap(da, True, 0), swap(db, True, 1)
    f32 = np.float32
    omegas = [f32(2.0 * math.pi) / (f32(16.0) + f32(32.0) * f32(i) / f32(nw)) for i in range(nw)]
    signals = [[f32(DT) * np.sin(f32(o * f32((k + 1) * DT))) for k in range(STEPS)] for o in omegas]
    cx, e1, e2, e3 = call(
        lambda *r: forward_body(*r, xl=xl, yl=yl, signals=signals), "forward",
        [(yr, xr, nz), field, field, field], [smem, smem] + [vmem] * 9,
        [ext(*field), ext(*field), ext(yr, xr, nz)],
    )(source_layer, monitor_layer, fe, fh, co, prof_t, rfa, rfb, rx, rda, rdb)
    last_a, grad = call(
        lambda *r: adjoint_body(*r, xl=xl, yl=yl, omegas=omegas), "adjoint",
        [field, (xl, nz)], [smem] + [vmem] * 11, [ext(*field)],
    )(monitor_layer, ae, ah, cx, e1, e2, e3, raa, rab, rx, rda, rdb)
    terms = over_wl(grad)
    out_f, out_a = call(
        lambda *r: store_body(*r, xl=xl, yl=yl), "store", [flat[0].shape] * 2, [vmem] * 2)(e3, last_a)
    (gradient,) = call(
        lambda *r: sum_body(*r, owned=owned, xl=xl, yl=yl), "gather_sum",
        [(owned, yl, xl)], [vmem] * nw, [ext(128, xl)],
    )(*terms)
    block = (1, 3, xl, yl, nz)
    return (out_f.reshape(block), out_a.reshape(block), jnp.transpose(gradient, (0, 2, 1)))


def solution(mesh):
    field = P("wl", None, "gx", "gy", None)
    return jax.shard_map(
        per_device,
        mesh=mesh,
        in_specs=(field, field, field, field, P("gx", "gy", None), P("wl", "gx", "gy"),
                  P("wl", "gx", "gy"), P("wl"), P("wl")),
        out_specs=(field, field, P("wl", "gx", "gy")),
        check_vma=False,
    )
```

```python
import math

import jax
import jax.numpy as jnp
import numpy as np
from jax import lax
from jax.experimental import pallas as pl
from jax.experimental.pallas import tpu as pltpu
from jax.sharding import PartitionSpec as P

Z0 = 64
STEPS = 3
DT = 0.5
F32 = jnp.float32
BF16 = jnp.bfloat16
FH = 5
AH = 3
WIN = 7
PER = 128 // WIN
PROF = 120


def swap(block, flip_x, parity):
    nx, ny = lax.axis_size("gx"), lax.axis_size("gy")
    route = []
    for a in range(nx):
        for b in range(ny):
            ta = a ^ 1 if flip_x else a
            tb = b if parity is None else ((b + parity) ^ 1) - parity
            if 0 <= ta < nx and 0 <= tb < ny:
                route.append((a * ny + b, ta * ny + tb))
    return lax.ppermute(block, ("gx", "gy"), route)


FWD, ADJ = ("fe", "fh"), ("ae", "ah")
def side_parts(e, h):
    return [(e, c, i) for c in range(3) for i in range(2)] + [(h, c, i) for c in range(3) for i in range(2)] + [(h, 0, 2), (h, 2, 2)]


CO_RAW, CO_WIN = [("co", 0, i) for i in (0, 1)], [("co", 0, i) for i in (2, 3)]
F_RAW = side_parts(*FWD) + CO_RAW
A_RAW = side_parts(*ADJ)
F_WIN = [("fe", c, i) for c in range(3) for i in (2, 3, 4)] + [("fh", 1, 2)]
F_WIN += [("fh", c, 3) for c in range(3)] + [("fh", 0, 4), ("fh", 2, 4)] + CO_WIN
C_RAW = side_parts(*FWD) + [("fe", 1, 2)] + A_RAW + [("ae", 1, 2)] + CO_RAW
C_WIN = [(n, c, i) for n in FWD for c in range(3) for i in range(FH)] + CO_RAW + CO_WIN


def x_parts(yl):
    raw = [(n, c, y) for n in FWD + ADJ for c in range(3) for y in range(yl)]
    win = [(n, c, y) for n in FWD for c in range(3) for y in range(yl)]
    co = [("co", 0, y) for y in range(yl)]
    return raw + co, win + co


def ceil(a, b):
    return -(-a // b)


def stepped(e, h, out, xl, yl):
    sub = lax.broadcasted_iota(jnp.int32, (xl, 128), 0)
    x_last = sub == xl - 1
    z_last = lax.broadcasted_iota(jnp.int32, (xl, 128), 1) == 127
    zup = lambda v: jnp.where(z_last, 0.0, pltpu.roll(v, 127, 1)) - v
    xup = lambda v: jnp.where(x_last, 0.0, pltpu.roll(v, xl - 1, 0)) - v
    row = lambda ref, c, y: ref[pl.ds(c * xl * yl + y, xl, stride=yl), :]
    cur = [row(e, c, 0) for c in range(3)]
    for y in range(yl - 1):
        up = [row(e, c, y + 1) for c in range(3)]
        ex, ey, ez = cur
        out[0, y] = row(h, 0, y) - DT * ((up[2] - ez) - zup(ey))
        out[1, y] = row(h, 1, y) - DT * (zup(ex) - xup(ez))
        out[2, y] = row(h, 2, y) - DT * (xup(ey) - (up[0] - ex))
        cur = up


def edge_row(e, h, h1, is_h, c, i, up, x, count, xl, yl):
    here = jnp.where(up, yl - 1 - i, i)
    flat = lambda ref, r: ref[pl.ds(c * xl * yl + x * yl + r, count, stride=yl), :]
    if not is_h:
        return flat(e, here)
    if i in (1, 2):
        return h1[c, here, pl.ds(x, count), :]
    return jnp.where(up, flat(h, yl - 1 - i), h1[c, i, pl.ds(x, count), :])


def fetch_body(ae, ah, fe, fh, bg, sp, *rest, xl, yl):
    outs, (h1, fh1, aa, ab, prof_t, turn, sems) = rest[:5], rest[5:]
    copies = [pltpu.make_async_copy(s, d, sems.at[i]) for i, (s, d) in enumerate(zip((ae, ah, fe, fh, bg), outs))]
    for c in copies:
        c.start()
    turn[...] = jnp.zeros((128, 128), F32)
    turn[0:yl, 0:xl] = sp[...]
    prof_t[...] = jnp.transpose(turn[...])[0:xl]
    copies[0].wait()
    copies[1].wait()
    e, h = outs[0], outs[1]
    gy = lax.axis_index("gy")
    stepped(e, h, h1, xl, yl)
    for u, (name, c, i) in enumerate(A_RAW):
        for dst, up in ((aa, gy % 2 == 0), (ab, gy % 2 == 1)):
            dst[u] = edge_row(e, h, h1, name == "ah", c, i, up, 0, xl, xl, yl)
    copies[2].wait()
    copies[3].wait()
    stepped(outs[2], outs[3], fh1, xl, yl)
    copies[4].wait()


def send_body(mon, fe, fh, ae, ah, bg, fh1, ah1, prof_t, *rest, xl, yl, nw, owned):
    parts, (co, fa, fb, px, da, db, turn) = rest[:nw], rest[nw:]
    gx, gy, w = lax.axis_index("gx"), lax.axis_index("gy"), lax.axis_index("wl")
    plane = xl * yl
    depth = nw * owned
    lane = lax.broadcasted_iota(jnp.int32, (xl, 128), 1)
    lane8 = lane[0:8]
    first = WIN // 2 - mon[0] + 256
    refs = dict(fe=fe, fh=fh, ae=ae, ah=ah)
    turn[...] = jnp.zeros((128, 128), F32)
    for k in range(nw):
        for i in range(owned):
            turn[pl.ds(owned * (w ^ k) + i, yl, stride=depth), 0:xl] = parts[k][i]
    layers = jnp.transpose(turn[...])[0:xl]
    for y in range(yl):
        moved = pltpu.roll(layers, (Z0 - depth * y) % 128, 1)
        perm = jnp.where((lane >= Z0) & (lane < Z0 + depth), moved, bg[pl.ds(y, xl, stride=yl), :])
        co[y] = DT / perm
    low_x = gx == 0
    x8 = pl.multiple_of(jnp.where(low_x, xl - 8, 0), 8)

    def beside(name, c, y, x, count):
        if name == "co":
            return co[y, pl.ds(x, count), :]
        return refs[name][pl.ds(c * plane + x * yl + y, count, stride=yl), :]

    def beyond(up):
        def rows(name, c, i, x, count):
            if name == "co":
                return co[jnp.where(up, yl - 1 - i, i), pl.ds(x, count), :]
            e, h, h1 = (fe, fh, fh1) if name in FWD else (ae, ah, ah1)
            return edge_row(e, h, h1, name in ("fh", "ah"), c, i, up, x, count, xl, yl)
        return rows

    def windows(parts, x, count, rows):
        out = []
        here = lax.broadcasted_iota(jnp.int32, (count, 128), 1)
        for t in range(ceil(len(parts), PER)):
            acc = jnp.zeros((count, 128), F32)
            for q, (name, c, i) in enumerate(parts[t * PER : (t + 1) * PER]):
                moved = pltpu.roll(rows(name, c, i, x, count), (WIN * q + first) % 128, 1)
                acc = jnp.where((here >= WIN * q) & (here < WIN * (q + 1)), moved, acc)
            out.append(acc)
        return out

    def tiles(dst, raw, win, rows):
        for n, (name, c, i) in enumerate(raw):
            half = pltpu.roll(rows(name, c, i, x8, 8), jnp.where(low_x, 4, 0), 0)[0:4]
            dst[n // 2, 4 * (n % 2) : 4 * (n % 2) + 4, :] = half
        at = ceil(len(raw), 2)
        for tile in windows(win, x8, 8, rows):
            dst[at] = tile
            at += 1
        return at

    for dst, corner, up in ((fa, da, gy % 2 == 0), (fb, db, gy % 2 == 1)):
        rows = beyond(up)
        for u, (name, c, i) in enumerate(F_RAW):
            dst[u] = rows(name, c, i, 0, xl)
        at = len(F_RAW)
        for unit in windows(F_WIN, 0, xl, rows):
            dst[at] = unit
            at += 1
        mix = dst[at - 1]
        prof = prof_t[...]
        for i in range(FH):
            col = jnp.where(up, prof[:, yl - 1 - i : yl - i], prof[:, i : i + 1])
            mix = jnp.where(lane == PROF + i, jnp.broadcast_to(col, (xl, 128)), mix)
        dst[at - 1] = mix
        last = tiles(corner, C_RAW, C_WIN, rows)
        src8 = dst[at - 1, pl.ds(x8, 8), :]
        corner[last - 1] = jnp.where((lane8 >= PROF) & (lane8 < PROF + FH), src8, corner[last - 1])
    raw, win = x_parts(yl)
    last = tiles(px, raw, win, beside)
    px[last] = prof_t[pl.ds(x8, 8), :]


class Halo:
    def __init__(self, mon, xl, yl, put):
        self.xl, self.yl, self.put = xl, yl, put
        self.gx, self.gy = lax.axis_index("gx"), lax.axis_index("gy")
        self.back = mon - WIN // 2 + 256
        sub = lax.broadcasted_iota(jnp.int32, (8, 128), 0)
        low = self.gx == 0
        mask = lambda lo, hi: jnp.where(low, lo.astype(F32), hi.astype(F32))
        self.keep = mask(sub < FH, sub >= 8 - FH)
        self.near = mask(sub < 4, sub >= 4) > 0.5
        self.far = mask((sub >= 4) & (sub < FH), (sub < 4) & (sub >= 8 - FH)) > 0.5
        self.shift = [jnp.where(low, 0, 4), jnp.where(low, 4, 0)]

    def row(self, i, high):
        return jnp.where(high, FH + self.yl + i, FH - 1 - i)

    def unroll(self, tile, q):
        return pltpu.roll(tile, (self.back - WIN * q) % 128, 1)

    def side(self, ref, raw, win, high):
        own = pl.ds(0, self.xl)
        for u, (name, c, i) in enumerate(raw):
            self.put(name, c, self.row(i, high), own, ref[u])
        for s, (name, c, i) in enumerate(win):
            self.put(name, c, self.row(i, high), own, self.unroll(ref[len(raw) + s // PER], s % PER))

    def tiles(self, ref, raw, win, names, where):
        halo = pl.ds(self.xl, 8)
        seats = {part: s for s, part in enumerate(win)}
        at = ceil(len(raw), 2)
        for n, part in enumerate(raw):
            if part[0] not in names:
                continue
            value = jnp.where(self.near, pltpu.roll(ref[n // 2], self.shift[n % 2], 0), 0.0)
            if part in seats:
                s = seats.pop(part)
                value = jnp.where(self.far, self.unroll(ref[at + s // PER], s % PER), value)
            self.put(part[0], part[1], where(part[2]), halo, value)
        for part, s in seats.items():
            if part[0] in names:
                self.put(part[0], part[1], where(part[2]), halo, self.unroll(ref[at + s // PER], s % PER) * self.keep)


class Stepper:
    def __init__(self, xl, yl, cx):
        self.xr = xr = xl + 8
        self.cx = cx
        gx, gy = lax.axis_index("gx"), lax.axis_index("gy")
        self.lane = lax.broadcasted_iota(jnp.int32, (xr, 128), 1)
        ring = lax.broadcasted_iota(jnp.int32, (xr, 128), 0)
        inside_low = jnp.where(ring < xl + FH, F32(DT), F32(0.0))
        inside_high = jnp.where((ring < xl) | (ring >= xr - FH), F32(DT), F32(0.0))
        self.h_in = jnp.where(gx == 0, inside_low, inside_high)
        self.h_low = self.h_in * jnp.where(gy == 0, 0.0, 1.0).astype(F32)
        edge = ((ring == xl - 1) | (ring == xr - 1)).astype(F32)
        self.h_edge = self.h_in * edge
        self.z_last = self.lane == 127
        ri = lax.broadcasted_iota(jnp.int32, (128, 128), 0)
        ci = lax.broadcasted_iota(jnp.int32, (128, 128), 1)
        diff = jnp.where(ri == ci, F32(1.0), F32(0.0)) - jnp.where(ri == ci - 1, F32(1.0), F32(0.0))
        self.diff = jnp.concatenate([diff] * 3, 0).astype(BF16)

    def zdn(self, p, q):
        v = jnp.concatenate([p, q], 0)
        hi = v.astype(BF16)
        rest = v - hi.astype(F32)
        mid = rest.astype(BF16)
        low = (rest - mid.astype(F32)).astype(BF16)
        out = lax.dot_general(jnp.concatenate([hi, mid, low], 1), self.diff, (((1,), (0,)), ((), ())),
                              preferred_element_type=F32)
        return out[0 : self.xr], out[self.xr :]

    def zup(self, v):
        return jnp.where(self.z_last, 0.0, pltpu.roll(v, 127, 1)) - v

    def xup(self, v):
        return pltpu.roll(v, self.xr - 1, 0) - v

    def xdn(self, v):
        return v - pltpu.roll(v, 1, 0)

    def rows(self, e, h, start, stop, given=()):
        load = lambda ref, y: (ref[0, y], ref[1, y], ref[2, y])
        cur, now = load(e, start), None
        for y in range(start, stop):
            up = load(e, y + 1)
            below = now
            k = self.h_low if y < FH else self.h_in
            ex, ey, ez = cur
            if y in given:
                k = self.h_edge
                now = (
                    h[0, y],
                    h[1, y] + k * pltpu.roll(ez, self.xr - 1, 0),
                    h[2, y] - k * pltpu.roll(ey, self.xr - 1, 0),
                )
            else:
                now = (
                    h[0, y] - k * ((up[2] - ez) - self.zup(ey)),
                    h[1, y] - k * (self.zup(ex) - self.xup(ez)),
                    h[2, y] - k * (self.xup(ey) - (up[0] - ex)),
                )
            for c in range(3):
                h[c, y] = now[c]
            if y > start:
                hx, hy, hz = now
                k = self.cx[y]
                zy, zx = self.zdn(hy, hx)
                yield y, cur, (
                    k * ((hz - below[2]) - zy),
                    k * (zx - self.xdn(hz)),
                    k * (self.xdn(hy) - (hx - below[0])),
                )
            cur = up


def given_rows(yl):
    return {FH - 3, FH - 2, *range(FH + yl, yl + 2 * FH)}


def pick(values):
    w = lax.axis_index("wl")
    value = F32(values[0])
    for i in range(1, len(values)):
        value = jnp.where(w == i, F32(values[i]), value)
    return value


def fill_own(refs, bigs, xl, yl):
    for ref, big in zip(refs, bigs):
        for c in range(3):
            for y in range(yl):
                big[c, FH + y, 0:xl, :] = ref[pl.ds(c * xl * yl + y, xl, stride=yl), :]


def put_out(big, out, xl, yl):
    for c in range(3):
        for y in range(yl):
            out[pl.ds(c * xl * yl + y, xl, stride=yl), :] = big[c, FH + y, 0:xl, :]


def store_body(e3, a, out_f, out_a, *, xl, yl):
    put_out(e3, out_f, xl, yl)
    put_out(a, out_a, xl, yl)


def forward_body(src, mon, fe, fh, co, prof_t, ra, rb, rx, rda, rdb, cx, e1, e2, e3, e0, h, sx, *, xl, yl, signals):
    xr, yr = xl + 8, yl + 2 * FH
    gy = lax.axis_index("gy")
    src_l = src[0]
    own, halo = pl.ds(0, xl), pl.ds(xl, 8)

    def put(name, c, row, cols, value):
        if name == "co":
            cx[row, cols, :] = value
        else:
            (e0 if name == "fe" else h)[c, row, cols, :] = value

    to = Halo(mon[0], xl, yl, put)
    fill_own((fe, fh), (e0, h), xl, yl)
    for y in range(yl):
        cx[FH + y, own, :] = co[y]
    names = FWD + ("co",)
    raw, win = x_parts(yl)
    to.tiles(rx, raw, win, names, lambda y: FH + y)
    at_src = lax.broadcasted_iota(jnp.int32, (xl, 128), 1) == src_l
    at_src8 = lax.broadcasted_iota(jnp.int32, (8, 128), 1) == src_l

    def source(row, wide, tile, lane):
        sx[row, own, :] = jnp.where(at_src, jnp.broadcast_to(wide[:, lane : lane + 1], (xl, 128)), 0.0)
        sx[row, halo, :] = jnp.where(at_src8, jnp.broadcast_to(tile[:, lane : lane + 1], (8, 128)), 0.0)

    prof, prof_x = prof_t[...], rx[rx.shape[0] - 1] * to.keep
    for y in range(yl):
        source(FH + y, prof, prof_x, y)
    for ref, ref_d, high in ((ra, rda, gy % 2 == 0), (rb, rdb, gy % 2 == 1)):
        to.side(ref, F_RAW, F_WIN, high)
        to.tiles(ref_d, C_RAW, C_WIN, names, lambda i, high=high: to.row(i, high))
        prof_y, prof_d = ref[ref.shape[0] - 1], ref_d[ref_d.shape[0] - 1] * to.keep
        for i in range(FH):
            source(to.row(i, high), prof_y, prof_d, PROF + i)
    step = Stepper(xl, yl, cx)
    runs = (e0, e1, e2, e3)
    for k in range(STEPS):
        new = runs[k + 1]
        signal = pick([s[k] for s in signals])
        for y, cur, inc in step.rows(runs[k], h, k, yr - 1 - k, given_rows(yl) if k == 0 else ()):
            new[0, y] = cur[0] + inc[0] + signal * sx[y]
            new[1, y] = cur[1] + inc[1]
            new[2, y] = cur[2] + inc[2]


def adjoint_body(mon, ae, ah, cx, e1, e2, e3, ra, rb, rx, rda, rdb, a, grad, g, *, xl, yl, omegas):
    yr = yl + 2 * FH
    gy = lax.axis_index("gy")

    def put(name, c, row, cols, value):
        (a if name == "ae" else g)[c, row, cols, :] = value

    to = Halo(mon[0], xl, yl, put)
    for c in range(3):
        a[c, FH - AH] = jnp.zeros((xl + 8, 128), F32)
    fill_own((ae, ah), (a, g), xl, yl)
    raw, win = x_parts(yl)
    to.tiles(rx, raw, win, ADJ, lambda y: FH + y)
    for ref, ref_d, high in ((ra, rda, gy % 2 == 0), (rb, rdb, gy % 2 == 1)):
        to.side(ref, A_RAW, [], high)
        to.tiles(ref_d, C_RAW, C_WIN, ADJ, lambda i, high=high: to.row(i, high))
    step = Stepper(xl, yl, cx)
    at_mon = step.lane == mon[0]
    total = [None] * yl
    for j in range(STEPS):
        seen = (e3, e2, e1)[j]
        for y, cur, inc in step.rows(a, g, FH - AH + j, yr - AH - j, given_rows(yl) if j == 0 else ()):
            for c in range(3):
                f = seen[c, y]
                v = cur[c] + inc[c] + jnp.where(at_mon, 2.0 * DT * f, 0.0)
                a[c, y] = v
                if FH <= y < FH + yl:
                    t = (f * v)[0:xl]
                    i = y - FH
                    total[i] = t if total[i] is None else total[i] + t
    scale = pick([o * o for o in omegas])
    lane = step.lane[0:xl]
    packed = jnp.zeros((xl, 128), F32)
    wide = 128 // yl
    for y in range(yl):
        moved = pltpu.roll(total[y] * scale, (wide * y - Z0) % 128, 1)
        packed = jnp.where((lane >= wide * y) & (lane < wide * (y + 1)), moved, packed)
    grad[...] = packed


def sum_body(*refs, owned, xl, yl):
    *parts, out, turn = refs
    w = lax.axis_index("wl")
    acc = parts[0][...]
    for p in parts[1:]:
        acc = acc + p[...]
    turn[...] = jnp.transpose(acc)
    for i in range(owned):
        out[i] = turn[pl.ds(owned * w + i, yl, stride=128 // yl), :]


def per_device(fe, fh, ae, ah, background, design, source_profile, source_layer, monitor_layer):
    _, _, xl, yl, nz = fe.shape
    nw = lax.axis_size("wl")
    owned = design.shape[0]
    xr, yr = xl + 8, yl + 2 * FH
    flat = [v.reshape(3 * xl * yl, nz) for v in (fe, fh, ae, ah)] + [background.reshape(xl * yl, nz)]
    sp = jnp.transpose(source_profile[0])
    shape = lambda *s: jax.ShapeDtypeStruct(s, F32)
    smem = pl.BlockSpec(memory_space=pltpu.SMEM)
    vmem = pl.BlockSpec(memory_space=pltpu.VMEM)
    hbm = pl.BlockSpec(memory_space=pltpu.HBM)
    ext = lambda *s: pltpu.VMEM(s, F32)
    field = (3, yr, xr, nz)

    def call(body, name, out, specs, scratch=()):
        return pl.pallas_call(
            body, out_shape=tuple(shape(*s) for s in out), in_specs=specs, out_specs=(vmem,) * len(out),
            scratch_shapes=list(scratch), name=name,
            compiler_params=pltpu.CompilerParams(vmem_limit_bytes=20 * 1024 * 1024),
        )

    def over_wl(v):
        return [v] + [lax.ppermute(v, "wl", [(i, i ^ k) for i in range(nw)]) for k in range(1, nw)]

    raw, win = x_parts(yl)
    f_side = (len(F_RAW) + ceil(len(F_WIN), PER), xl, nz)
    a_side = (len(A_RAW), xl, nz)
    corner = (ceil(len(C_RAW), 2) + ceil(len(C_WIN), PER), 8, nz)
    beside = (ceil(len(raw), 2) + ceil(len(win), PER) + 1, 8, nz)

    layers = over_wl(jnp.transpose(design, (0, 2, 1)))
    fe, fh, ae, ah, bg = flat
    h1 = (3, yl, xl, nz)
    ae, ah, fe, fh, bg, ah1, fh1, aa, ab, prof_t = call(
        lambda *r: fetch_body(*r, xl=xl, yl=yl), "fetch",
        [ae.shape] * 4 + [bg.shape, h1, h1, a_side, a_side, (xl, nz)], [hbm] * 5 + [vmem],
        [ext(128, 128), pltpu.SemaphoreType.DMA((5,))],
    )(*[pltpu.with_memory_space_constraint(v, pltpu.HBM) for v in (ae, ah, fe, fh, bg)], sp)
    raa, rab = swap(aa, False, 0), swap(ab, False, 1)
    co, fa, fb, px, da, db = call(
        lambda *r: send_body(*r, xl=xl, yl=yl, nw=nw, owned=owned), "send",
        [(yl, xl, nz), f_side, f_side, beside, corner, corner],
        [smem] + [vmem] * (8 + nw), [ext(128, 128)],
    )(monitor_layer, fe, fh, ae, ah, bg, fh1, ah1, prof_t, *layers)
    rfa, rfb = swap(fa, False, 0), swap(fb, False, 1)
    rx = swap(px, True, None)
    rda, rdb = swap(da, True, 0), swap(db, True, 1)
    f32 = np.float32
    omegas = [f32(2.0 * math.pi) / (f32(16.0) + f32(32.0) * f32(i) / f32(nw)) for i in range(nw)]
    signals = [[f32(DT) * np.sin(f32(o * f32((k + 1) * DT))) for k in range(STEPS)] for o in omegas]
    cx, e1, e2, e3 = call(
        lambda *r: forward_body(*r, xl=xl, yl=yl, signals=signals), "forward",
        [(yr, xr, nz), field, field, field], [smem, smem] + [vmem] * 9,
        [ext(*field), ext(*field), ext(yr, xr, nz)],
    )(source_layer, monitor_layer, fe, fh, co, prof_t, rfa, rfb, rx, rda, rdb)
    last_a, grad = call(
        lambda *r: adjoint_body(*r, xl=xl, yl=yl, omegas=omegas), "adjoint",
        [field, (xl, nz)], [smem] + [vmem] * 11, [ext(*field)],
    )(monitor_layer, ae, ah, cx, e1, e2, e3, raa, rab, rx, rda, rdb)
    terms = over_wl(grad)
    out_f, out_a = call(
        lambda *r: store_body(*r, xl=xl, yl=yl), "store", [flat[0].shape] * 2, [vmem] * 2)(e3, last_a)
    (gradient,) = call(
        lambda *r: sum_body(*r, owned=owned, xl=xl, yl=yl), "gather_sum",
        [(owned, yl, xl)], [vmem] * nw, [ext(128, xl)],
    )(*terms)
    block = (1, 3, xl, yl, nz)
    return (out_f.reshape(block), out_a.reshape(block), jnp.transpose(gradient, (0, 2, 1)))


def solution(mesh):
    field = P("wl", None, "gx", "gy", None)
    return jax.shard_map(
        per_device,
        mesh=mesh,
        in_specs=(field, field, field, field, P("gx", "gy", None), P("wl", "gx", "gy"),
                  P("wl", "gx", "gy"), P("wl"), P("wl")),
        out_specs=(field, field, P("wl", "gx", "gy")),
        check_vma=False,
    )
```
